256 devices in a mesh: expert: 32 (over y, z), unit: 8 (over x, core).
Axes of the slice: x: 4, y: 4, z: 8, core: 2. Of those that a mesh axis runs over, the one named last changes fastest.
Arguments:
- w_up: bfloat16 [128, 1536, 4096], P('expert', 'unit'), may hold values from -0.09375 to 0.09375
- cluster: int32 [128, 1], replicated, may hold values from 0 to 31
- counts: int32 [128], replicated, may hold values from 16 to 127
Outputs:
- merged: bfloat16 [32, 1536, 4096], P('expert', None, 'unit')
The draws below stay inside these ranges and needn't reach their ends.
Inputs may be any that keep to these rules, and one draw needn't show every extreme that they name: Every cluster has at least one member.
All inputs are finite; a program needn't handle non-finite values.
Results may differ from the reference program's by a relative error of at most 0.0051.
Values may be sent and summed in bfloat16 or wider, within the bound.
No kernel may reach another device: no remote copies, remote signals or barrier semaphores. Data moves between devices by JAX's collectives and lax.ppermute only.
A program may use at most 128 MiB of HBM per device.

```python
import jax
import jax.numpy as jnp
from jax import lax

D = 4096
FF = 1536
BLOCK = 96
NS_STEPS = 8
EXPERTS = 128
CLUSTERS = 32


def with_ends(entries, key, least, high):
    index_at = [jax.random.randint(jax.random.fold_in(key, axis), (), 0, length) for axis, length in enumerate(entries.shape)]
    main_axis = entries.shape.index(max(entries.shape))
    beside = index_at[:main_axis] + [(index_at[main_axis] + 1) % entries.shape[main_axis]] + index_at[main_axis + 1:]
    return entries.at[tuple(index_at)].set(least).at[tuple(beside)].set(high)


def shard_levels(key, dims, split, low, largest):
    def one(position, shards_of):
        steps = jax.random.uniform(jax.random.fold_in(jax.random.fold_in(key, 6), position), (shards_of,), jnp.float32, low / len(split), largest / len(split))
        return jnp.repeat(jnp.exp(steps), dims[position] // shards_of).reshape((-1,) + (1,) * (len(dims) - position - 1))

    level = one(*split[0])
    for cut in split[1:]:
        level = level * one(*cut)
    return level


def choose_distinct(key, rows, number_of, top, lift):
    sequence = jax.random.permutation(jax.random.fold_in(key, 1), number_of)
    boost = sequence
    for power in range(3):
        boost = boost * boost // number_of
    boost = boost * lift // number_of
    tickets = jax.random.randint(jax.random.fold_in(key, 2), (rows, number_of), 0, 4096) + boost
    fixed_rows = jax.random.permutation(jax.random.fold_in(key, 3), rows)[jnp.arange(number_of) % rows]
    tickets = jnp.where(jnp.arange(rows)[:, None] == fixed_rows[None, :], 1 << 14, tickets)
    merit = tickets * number_of + jnp.arange(number_of)
    return lax.top_k(merit.astype(jnp.int32), top)[1].astype(jnp.int32)


def bell_draw(rng, dims, scale, bound, cuts=(), kind=jnp.bfloat16):
    gain = shard_levels(rng, dims, cuts, -0.22, 0.18) if cuts else 1.0
    drawn = jax.random.normal(rng, dims, jnp.float32) * scale * gain
    return jnp.minimum(jnp.maximum(drawn, -bound), bound).astype(kind)


def setup_inputs(seed: int = 0) -> dict:
    seeds = jax.random.split(jax.random.key(seed), 4)
    return {
        "w_up": bell_draw(seeds[0], (EXPERTS, FF, D), D ** -0.5, 0.09375, ((0, 32), (1, 8))),
        "cluster": choose_distinct(seeds[1], EXPERTS, CLUSTERS, 1, 512),
        "counts": with_ends(jax.random.randint(seeds[2], (EXPERTS,), 16, 128), jax.random.fold_in(seeds[2], 1), 16, 127).astype(jnp.int32),
    }


def newton_schulz(matrices):
    frob_norm = jnp.sqrt(lax.optimization_barrier(jnp.sum(matrices * matrices, axis=(-2, -1), keepdims=True)) + 1e-06)
    value = matrices / frob_norm
    for iteration in range(NS_STEPS):
        square = jnp.einsum('...ij,...kj->...ik', value, value, precision=lax.Precision.HIGHEST)
        value = 1.5 * value - 0.5 * jnp.einsum('...ik,...kj->...ij', square, value, precision=lax.Precision.HIGHEST)
    return value

def reference(w_up, cluster, counts):
    cluster_ids = cluster[:, 0]
    experts = cluster_ids.shape[0]
    index = jnp.arange(experts, dtype=jnp.int32)
    labels = jnp.arange(CLUSTERS, dtype=jnp.int32)
    member = cluster_ids[None, :] == labels[:, None]
    score = counts * experts + (experts - 1 - index)
    best = lax.optimization_barrier(jnp.max(jnp.where(member, score[None, :], -1), axis=1))
    leader = (experts - 1 - best % experts).astype(jnp.int32)
    anchor_of = leader[cluster_ids].astype(jnp.int32)
    total = lax.optimization_barrier(jnp.sum(jnp.where(member, counts[None, :], 0), axis=1)).astype(jnp.float32)
    weight = counts.astype(jnp.float32) / total[cluster_ids]
    nblocks = FF // BLOCK

    def one_expert(carry, which):
        member_rows = w_up[which].astype(jnp.float32).reshape(nblocks, BLOCK, D)
        lead_rows = w_up[anchor_of[which]].astype(jnp.float32).reshape(nblocks, BLOCK, D)
        gram = jnp.einsum('bid,bjd->bij', lead_rows, member_rows, precision=lax.Precision.HIGHEST)
        polar = newton_schulz(gram).astype(jnp.bfloat16)
        turned = jnp.einsum('bij,bjd->bid', polar.astype(jnp.float32), member_rows, precision=lax.Precision.HIGHEST)
        aligned = (turned * weight[which]).reshape(FF, D).astype(jnp.bfloat16)
        aligned = lax.optimization_barrier(aligned)
        carry = carry.at[cluster_ids[which]].add(aligned.astype(jnp.float32))
        return (carry, None)
    merged, unused = lax.scan(one_expert, jnp.zeros((CLUSTERS, FF, D), jnp.float32), index)
    return merged.astype(jnp.bfloat16)
```

```python
import jax
import jax.numpy as jnp
from jax import lax
from jax.experimental import pallas as pl
from jax.experimental.pallas import tpu as pltpu
from jax.sharding import Mesh, PartitionSpec as P

BLOCK = 96
NS_STEPS = 8
NY, NZ, NX, NC = 4, 8, 4, 2
EXPERTS = 128
CLUSTERS = 32
COLS = 256
VMEM = pl.BlockSpec(memory_space=pltpu.VMEM)
SMEM = pl.BlockSpec(memory_space=pltpu.SMEM)


def newton_schulz(matrices):
    frob_norm = jnp.sqrt(jnp.sum(matrices * matrices, axis=(-2, -1), keepdims=True) + 1e-06)
    value = matrices / frob_norm
    for iteration in range(NS_STEPS):
        square = jnp.einsum("...ij,...kj->...ik", value, value, precision=lax.Precision.HIGHEST)
        value = 1.5 * value - 0.5 * jnp.einsum(
            "...ik,...kj->...ij", square, value, precision=lax.Precision.HIGHEST
        )
    return value


def spread_kernel(w_ref, o_ref):
    for s in range(NZ * NC):
        o_ref[s % NC, 0, s // NC, 0] = w_ref[0, :, s * COLS:(s + 1) * COLS]


def spread(w):
    experts, units, width = w.shape
    return pl.pallas_call(
        spread_kernel,
        grid=(experts, units // BLOCK),
        in_specs=[pl.BlockSpec((1, BLOCK, width), lambda e, j: (e, j, 0))],
        out_specs=pl.BlockSpec((NC, 1, NZ, 1, BLOCK, COLS), lambda e, j: (0, j, 0, e, 0, 0)),
        out_shape=jax.ShapeDtypeStruct((NC, units // BLOCK, NZ, experts, BLOCK, COLS), w.dtype),
    )(w)


def gram_kernel(anchor_ref, core_ref, w_ref, keep_ref, send_ref):
    half = EXPERTS // NC
    core = core_ref[0]

    def one(m):
        return lax.dot_general(
            w_ref[anchor_ref[m]], w_ref[m], (((1,), (1,)), ((), ())), preferred_element_type=jnp.float32
        )

    def step(i, carry):
        keep_ref[i] = one(core * half + i)
        send_ref[i] = one((1 - core) * half + i)
        return carry

    lax.fori_loop(0, half, step, 0, unroll=4)


def grams(anchor_of, core, columns):
    shape = jax.ShapeDtypeStruct((EXPERTS // NC, BLOCK, BLOCK), jnp.float32)
    return pl.pallas_call(
        gram_kernel, in_specs=[SMEM, SMEM, VMEM], out_specs=[VMEM, VMEM], out_shape=[shape, shape]
    )(anchor_of, core, columns)


def align_kernel(slot_ref, weight_ref, polar_ref, w_ref, o_ref, acc_ref):
    acc_ref[...] = jnp.zeros_like(acc_ref)
    half = EXPERTS // NC

    def step(m, carry):
        place = ((m % half) // 8 * NC + m // half) * 8 + m % 8
        turned = jnp.dot(polar_ref[place], w_ref[m], preferred_element_type=jnp.float32)
        turned = (turned * weight_ref[m]).astype(jnp.bfloat16).astype(jnp.float32)
        slot = slot_ref[m]
        acc_ref[slot] = acc_ref[slot] + turned
        return carry

    lax.fori_loop(0, EXPERTS, step, 0, unroll=4)
    o_ref[...] = acc_ref[...].astype(o_ref.dtype)


def align(slot_of, weight, polar, columns):
    return pl.pallas_call(
        align_kernel,
        in_specs=[SMEM, SMEM, VMEM, VMEM],
        out_specs=VMEM,
        out_shape=jax.ShapeDtypeStruct((CLUSTERS, BLOCK, COLS), jnp.bfloat16),
        scratch_shapes=[pltpu.VMEM((CLUSTERS, BLOCK, COLS), jnp.float32)],
    )(slot_of, weight, polar, columns)


def on_device(w_up, cluster, counts):
    cluster_ids = cluster[:, 0]
    index = jnp.arange(EXPERTS, dtype=jnp.int32)
    labels = jnp.arange(CLUSTERS, dtype=jnp.int32)
    member = cluster_ids[None, :] == labels[:, None]
    score = counts * EXPERTS + (EXPERTS - 1 - index)
    best = jnp.max(jnp.where(member, score[None, :], -1), axis=1)
    leader = EXPERTS - 1 - best % EXPERTS
    anchor_of = jnp.sum(jnp.where(member, leader[:, None], 0), axis=0)
    total = jnp.sum(jnp.where(member, counts[None, :], 0), axis=1).astype(jnp.float32)
    weight = counts.astype(jnp.float32) / jnp.sum(jnp.where(member, total[:, None], 0.0), axis=0)
    slot_of = cluster_ids % NZ * NY + cluster_ids // NZ
    core = lax.axis_index("core").astype(jnp.int32).reshape(1)

    rows = spread(w_up)
    rows = lax.all_to_all(rows, "core", split_axis=0, concat_axis=0, tiled=True)
    rows = rows.reshape(NY * NZ, 4 * BLOCK, COLS)
    columns = lax.all_to_all(rows, ("y", "z"), split_axis=0, concat_axis=0, tiled=True)
    columns = columns.reshape(EXPERTS, BLOCK, COLS)

    keep, send = grams(anchor_of, core, columns)
    partial = keep + lax.ppermute(send, "core", [(0, 1), (1, 0)])
    gram = lax.psum_scatter(partial, "z", scatter_dimension=0, tiled=True)
    polar = newton_schulz(gram).astype(jnp.bfloat16)
    polar = lax.all_gather(polar, ("z", "core"), axis=0, tiled=True)
    merged = align(slot_of, weight, polar, columns)

    merged = lax.all_to_all(merged, ("z", "y"), split_axis=0, concat_axis=0, tiled=True)
    merged = merged.reshape(NZ, NY * BLOCK, COLS)
    merged = lax.all_to_all(merged, ("x", "core"), split_axis=0, concat_axis=0, tiled=True)
    merged = merged.reshape(NX, NC, NY * BLOCK, COLS).transpose(0, 2, 1, 3)
    return merged.reshape(1, NX * NY * BLOCK, NC * COLS)


def solution(mesh):
    grid = Mesh(mesh.devices.reshape(NY, NZ, NX, NC), ("y", "z", "x", "core"))
    return jax.shard_map(
        on_device,
        mesh=grid,
        in_specs=(P(("y", "z"), ("x", "core"), None), P(), P()),
        out_specs=P(("y", "z"), None, ("x", "core")),
        check_vma=False,
    )
```

```python
import jax
import jax.numpy as jnp
from jax import lax
from jax.experimental import pallas as pl
from jax.experimental.pallas import tpu as pltpu
from jax.sharding import Mesh, PartitionSpec as P

BLOCK = 96
NS_STEPS = 8
NY, NZB, NZC, NX, NC = 4, 4, 2, 4, 2
EXPERTS = 128
CLUSTERS = 32
COLS = 256
PACK = 4
LANES = PACK * BLOCK
SLICES = NY * NZC
GROUPS = EXPERTS // PACK // NC
MINE = GROUPS // SLICES
SWAP = [(0, 1), (1, 0)]
VMEM = pl.BlockSpec(memory_space=pltpu.VMEM)
SMEM = pl.BlockSpec(memory_space=pltpu.SMEM)


def flip(position):
    return ((position >> 3) & 3) * 32 + (position >> 5) * 8 + (position & 7)


def spread_kernel(core_ref, w_ref, o_ref, *, other):
    half = 1 - core_ref[0] if other else core_ref[0]
    for u in range(SLICES):
        start = pl.multiple_of((2 * u + half) * COLS, COLS)
        o_ref[0, u, 0] = w_ref[0, :, pl.ds(start, COLS)]


def spread(core, w, other):
    experts, units, width = w.shape
    blocks = units // BLOCK

    def kernel(core_ref, w_ref, o_ref):
        spread_kernel(core_ref, w_ref, o_ref, other=other)

    def place(e, j, core_ref):
        return (j if other else core_ref[0] * blocks + j, 0, e, 0, 0)

    return pl.pallas_call(
        kernel,
        grid_spec=pltpu.PrefetchScalarGridSpec(
            num_scalar_prefetch=1,
            grid=(experts, blocks),
            in_specs=[pl.BlockSpec((1, BLOCK, width), lambda e, j, core_ref: (e, j, 0))],
            out_specs=pl.BlockSpec((1, SLICES, 1, BLOCK, COLS), place),
        ),
        out_shape=jax.ShapeDtypeStruct((blocks if other else NC * blocks, SLICES, experts, BLOCK, COLS), w.dtype),
    )(core, w)


def join_kernel(core_ref, got_ref, held_ref, o_ref):
    o_ref[...] = got_ref[...]


def join(core, got, held):
    blocks, slices, experts, _, _ = got.shape
    block = (1, 2, experts, BLOCK, COLS)
    return pl.pallas_call(
        join_kernel,
        grid_spec=pltpu.PrefetchScalarGridSpec(
            num_scalar_prefetch=1,
            grid=(blocks, slices // 2),
            in_specs=[
                pl.BlockSpec(block, lambda j, u, core_ref: (j, u, 0, 0, 0)),
                pl.BlockSpec(memory_space=pl.ANY),
            ],
            out_specs=pl.BlockSpec(block, lambda j, u, core_ref: ((1 - core_ref[0]) * blocks + j, u, 0, 0, 0)),
        ),
        out_shape=jax.ShapeDtypeStruct(held.shape, held.dtype),
        input_output_aliases={2: 0},
    )(core, got, held)


def grams(anchor_of, core, columns, other):
    def kernel(anchor_ref, core_ref, w_ref, o_ref):
        half = 1 - core_ref[0] if other else core_ref[0]

        def step(g, carry):
            parts = []
            for i in range(PACK):
                p = (half * GROUPS + g) * PACK + i
                lead = flip(anchor_ref[flip(p)])
                parts.append(
                    lax.dot_general(
                        w_ref[lead], w_ref[p], (((1,), (1,)), ((), ())), preferred_element_type=jnp.float32
                    )
                )
            o_ref[g] = jnp.concatenate(parts, axis=1)
            return carry

        lax.fori_loop(0, GROUPS, step, 0)

    return pl.pallas_call(
        kernel,
        in_specs=[SMEM, SMEM, VMEM],
        out_specs=VMEM,
        out_shape=jax.ShapeDtypeStruct((GROUPS, BLOCK, LANES), jnp.float32),
    )(anchor_of, core, columns)


def polar_kernel(part_ref, o_ref, x_ref):
    count = MINE * PACK
    for g in range(MINE):
        total = part_ref[0, g]
        for s in range(1, SLICES):
            total = total + part_ref[s, g]
        for i in range(PACK):
            gram = total[:, i * BLOCK:(i + 1) * BLOCK]
            norm = jnp.sqrt(jnp.sum(jnp.sum(gram * gram, axis=1, keepdims=True), axis=0, keepdims=True) + 1e-06)
            x_ref[g * PACK + i] = gram / norm

    def step(it, carry):
        for n in range(count):
            x = x_ref[n]
            square = lax.dot_general(
                x, x, (((1,), (1,)), ((), ())),
                precision=lax.Precision.HIGHEST, preferred_element_type=jnp.float32,
            )
            cube = jnp.dot(square, x, precision=lax.Precision.HIGHEST, preferred_element_type=jnp.float32)
            x_ref[n] = 1.5 * x - 0.5 * cube
        return carry

    lax.fori_loop(0, NS_STEPS, step, 0)
    for g in range(MINE):
        packed = jnp.concatenate([x_ref[g * PACK + i] for i in range(PACK)], axis=1).astype(o_ref.dtype)
        for s in range(SLICES):
            o_ref[s, g] = packed


def polars(parts):
    return pl.pallas_call(
        polar_kernel,
        in_specs=[VMEM],
        out_specs=VMEM,
        out_shape=jax.ShapeDtypeStruct((SLICES, MINE, BLOCK, LANES), jnp.bfloat16),
        scratch_shapes=[pltpu.VMEM((MINE * PACK, BLOCK, BLOCK), jnp.float32)],
    )(parts)


def align_kernel(cluster_ref, weight_ref, core_ref, own_ref, got_ref, w_ref, o_ref, acc_ref):
    acc_ref[...] = jnp.zeros_like(acc_ref)
    core = core_ref[0]

    def step(g, carry):
        for half, ref in ((core, own_ref), (1 - core, got_ref)):
            packed = ref[g]
            for i in range(PACK):
                p = (half * GROUPS + g) * PACK + i
                m = flip(p)
                turned = jnp.dot(
                    packed[:, i * BLOCK:(i + 1) * BLOCK], w_ref[p], preferred_element_type=jnp.float32
                )
                turned = (turned * weight_ref[m]).astype(jnp.bfloat16).astype(jnp.float32)
                k = cluster_ref[m]
                slot = (k >> 3) * 8 + (k & 1) * 4 + ((k >> 1) & 3)
                acc_ref[slot] = acc_ref[slot] + turned
        return carry

    lax.fori_loop(0, GROUPS, step, 0)
    o_ref[...] = acc_ref[...].astype(o_ref.dtype)


def align(cluster_ids, weight, core, own, got, columns):
    return pl.pallas_call(
        align_kernel,
        in_specs=[SMEM, SMEM, SMEM, VMEM, VMEM, VMEM],
        out_specs=VMEM,
        out_shape=jax.ShapeDtypeStruct((CLUSTERS, BLOCK, COLS), jnp.bfloat16),
        scratch_shapes=[pltpu.VMEM((CLUSTERS, BLOCK, COLS), jnp.float32)],
    )(cluster_ids, weight, core, own, got, columns)


def final_kernel(m_ref, o_ref):
    for c in range(NC):
        o_ref[0, :, c * COLS:(c + 1) * COLS] = m_ref[0, c]


def final(merged):
    rows = merged.shape[2]
    return pl.pallas_call(
        final_kernel,
        grid=(NX,),
        in_specs=[pl.BlockSpec((1, NC, rows, COLS), lambda x: (x, 0, 0, 0))],
        out_specs=pl.BlockSpec((1, rows, NC * COLS), lambda x: (0, x, 0)),
        out_shape=jax.ShapeDtypeStruct((1, NX * rows, NC * COLS), merged.dtype),
    )(merged)


def exchange(value, axes):
    return lax.all_to_all(value, axes, split_axis=0, concat_axis=0, tiled=True)


def on_device(w_up, cluster, counts):
    cluster_ids = cluster[:, 0]
    index = jnp.arange(EXPERTS, dtype=jnp.int32)
    labels = jnp.arange(CLUSTERS, dtype=jnp.int32)
    member = cluster_ids[None, :] == labels[:, None]
    score = counts * EXPERTS + (EXPERTS - 1 - index)
    best = jnp.max(jnp.where(member, score[None, :], -1), axis=1)
    leader = EXPERTS - 1 - best % EXPERTS
    anchor_of = jnp.sum(jnp.where(member, leader[:, None], 0), axis=0)
    total = jnp.sum(jnp.where(member, counts[None, :], 0), axis=1).astype(jnp.float32)
    weight = counts.astype(jnp.float32) / jnp.sum(jnp.where(member, total[:, None], 0.0), axis=0)
    core = lax.axis_index("core").astype(jnp.int32).reshape(1)

    got = lax.ppermute(spread(core, w_up, True), "core", SWAP)
    rows = join(core, got, spread(core, w_up, False))
    rows = rows.reshape(NZB * SLICES, -1, COLS)
    columns = exchange(rows, ("zb", "y", "zc")).reshape(EXPERTS, BLOCK, COLS)

    got = lax.ppermute(grams(anchor_of, core, columns, True), "core", SWAP)
    partial = grams(anchor_of, core, columns, False) + got
    parts = exchange(partial, ("y", "zc"))
    copies = polars(parts.reshape(SLICES, MINE, BLOCK, LANES))
    own = exchange(copies, ("y", "zc")).reshape(GROUPS, BLOCK, LANES)
    merged = align(cluster_ids, weight, core, own, lax.ppermute(own, "core", SWAP), columns)

    merged = exchange(merged, ("y", "zc", "zb"))
    merged = exchange(merged.reshape(SLICES, NZB * BLOCK, COLS), ("x", "core"))
    return final(merged.reshape(NX, NC, NZB * BLOCK, COLS))


def solution(mesh):
    grid = Mesh(mesh.devices.reshape(NY, NZB, NZC, NX, NC), ("y", "zb", "zc", "x", "core"))
    return jax.shard_map(
        on_device,
        mesh=grid,
        in_specs=(P(("y", "zb", "zc"), ("x", "core"), None), P(), P()),
        out_specs=P(("y", "zb", "zc"), None, ("x", "core")),
        check_vma=False,
    )
```

```python
import jax
import jax.numpy as jnp
from jax import lax
from jax.experimental import pallas as pl
from jax.experimental.pallas import tpu as pltpu
from jax.sharding import Mesh, PartitionSpec as P

BLOCK = 96
NS_STEPS = 8
NY, NZB, NZC, NX, NC = 4, 4, 2, 4, 2
EXPERTS = 128
CLUSTERS = 32
COLS = 256
PACK = 4
LANE = 128
LANES = PACK * BLOCK
SLICES = NY * NZC
GROUPS = EXPERTS // PACK // NC
MINE = GROUPS // SLICES
SWAP = [(0, 1), (1, 0)]
VMEM = pl.BlockSpec(memory_space=pltpu.VMEM)
SMEM = pl.BlockSpec(memory_space=pltpu.SMEM)
ANY = pl.BlockSpec(memory_space=pl.ANY)
NT = (((1,), (1,)), ((), ()))
SMALL = pltpu.CompilerParams(vmem_limit_bytes=20 * 2**20)


def flip(position):
    return ((position >> 3) & 3) * 32 + (position >> 5) * 8 + (position & 7)


def quarters(parts):
    lane = lax.broadcasted_iota(jnp.int32, parts[0].shape, 1)
    low = lane < 64
    even = (lane // 32) % 2 == 0
    first = [jnp.where(low, parts[t], pltpu.roll(parts[t + 2], 64, 1)) for t in range(2)]
    second = [jnp.where(low, pltpu.roll(parts[t], 64, 1), parts[t + 2]) for t in range(2)]
    out = []
    for one, two in (first, second):
        out.append(jnp.where(even, one, pltpu.roll(two, 32, 1)))
        out.append(jnp.where(even, pltpu.roll(one, 96, 1), two))
    return out


def spread_kernel(core_ref, w_ref, held_ref, send_ref):
    def go(core):
        for h in range(2):
            for a in range(4):
                starts = [(4 * h + t) * 4 * LANE + a * LANE for t in range(4)]
                pieces = quarters([w_ref[0, :, s:s + LANE] for s in starts])
                for b in range(4):
                    ref = held_ref if b % 2 == core else send_ref
                    ref[0, 2 * a + b // 2, 0, :, h * LANE:(h + 1) * LANE] = pieces[b]

    for core in range(NC):
        pl.when(core_ref[0] == core)(lambda core=core: go(core))


def spread(core, w):
    experts, units, width = w.shape
    blocks = units // BLOCK
    block = (1, SLICES, 1, BLOCK, COLS)
    return pl.pallas_call(
        spread_kernel,
        compiler_params=SMALL,
        grid_spec=pltpu.PrefetchScalarGridSpec(
            num_scalar_prefetch=1,
            grid=(experts, blocks),
            in_specs=[pl.BlockSpec((1, BLOCK, width), lambda e, j, core_ref: (e, j, 0))],
            out_specs=[
                pl.BlockSpec(block, lambda e, j, core_ref: (core_ref[0] * blocks + j, 0, e, 0, 0)),
                pl.BlockSpec(block, lambda e, j, core_ref: (j, 0, e, 0, 0)),
            ],
        ),
        out_shape=[
            jax.ShapeDtypeStruct((NC * blocks, SLICES, experts, BLOCK, COLS), w.dtype),
            jax.ShapeDtypeStruct((blocks, SLICES, experts, BLOCK, COLS), w.dtype),
        ],
    )(core, w)


def join_kernel(core_ref, got_ref, held_ref, o_ref, sem):
    blocks = got_ref.shape[0]
    copy = pltpu.make_async_copy(got_ref, o_ref.at[pl.ds((1 - core_ref[0]) * blocks, blocks)], sem)
    copy.start()
    copy.wait()


def join(core, got, held):
    return pl.pallas_call(
        join_kernel,
        compiler_params=SMALL,
        in_specs=[SMEM, ANY, ANY],
        out_specs=ANY,
        out_shape=jax.ShapeDtypeStruct(held.shape, held.dtype),
        scratch_shapes=[pltpu.SemaphoreType.DMA],
        input_output_aliases={2: 0},
    )(core, got, held)


def grams(anchor_of, core, columns, other):
    def kernel(anchor_ref, core_ref, w_ref, o_ref):
        half = 1 - core_ref[0] if other else core_ref[0]

        def step(g, carry):
            parts = []
            for i in range(PACK):
                p = (half * GROUPS + g) * PACK + i
                lead = flip(anchor_ref[flip(p)])
                parts.append(lax.dot_general(w_ref[lead], w_ref[p], NT, preferred_element_type=jnp.float32))
            o_ref[g] = jnp.concatenate(parts, axis=1)
            return carry

        lax.fori_loop(0, GROUPS, step, 0, unroll=4)

    return pl.pallas_call(
        kernel,
        compiler_params=SMALL,
        in_specs=[SMEM, SMEM, VMEM],
        out_specs=VMEM,
        out_shape=jax.ShapeDtypeStruct((GROUPS, BLOCK, LANES), jnp.float32),
    )(anchor_of, core, columns)


def split(value):
    high = value.astype(jnp.bfloat16)
    return high, (value - high.astype(jnp.float32)).astype(jnp.bfloat16)


def fold(product):
    return product[:BLOCK, :LANE] + product[BLOCK:, :LANE] + product[:BLOCK, LANE:]


def polar_kernel(part_ref, o_ref, x_ref):
    count = MINE * PACK
    for g in range(MINE):
        total = part_ref[0, g]
        for s in range(1, SLICES):
            total = total + part_ref[s, g]
        for i in range(PACK):
            gram = total[:, i * BLOCK:(i + 1) * BLOCK]
            gram = jnp.concatenate([gram, jnp.zeros((BLOCK, LANE - BLOCK), jnp.float32)], axis=1)
            norm = jnp.sqrt(jnp.sum(jnp.sum(gram * gram, axis=1, keepdims=True), axis=0, keepdims=True) + 1e-06)
            x_ref[g * PACK + i] = gram / norm
    pad = jnp.zeros((LANE - BLOCK, LANE), jnp.bfloat16)

    def square(high, low):
        return lax.dot_general(
            jnp.concatenate([high, low], 0), jnp.concatenate([high, pad, low, pad], 0), NT,
            preferred_element_type=jnp.float32,
        )

    def times(one, two):
        wide = jnp.concatenate([jnp.concatenate([part, pad], 0) for part in two], 1)
        return jnp.dot(jnp.concatenate(one, 0), wide, preferred_element_type=jnp.float32)

    def step(it, carry):
        values = [x_ref[n] for n in range(count)]
        halves = [split(v) for v in values]
        squares = [split(fold(square(*v))) for v in halves]
        cubes = [times(s, v) for s, v in zip(squares, halves)]
        for n in range(count):
            x_ref[n] = 1.5 * values[n] - 0.5 * fold(cubes[n])
        return carry

    lax.fori_loop(0, NS_STEPS, step, 0)
    for g in range(MINE):
        packed = jnp.concatenate([x_ref[g * PACK + i][:, :BLOCK] for i in range(PACK)], axis=1).astype(o_ref.dtype)
        for s in range(SLICES):
            o_ref[s, g] = packed


def polars(parts):
    return pl.pallas_call(
        polar_kernel,
        compiler_params=SMALL,
        in_specs=[VMEM],
        out_specs=VMEM,
        out_shape=jax.ShapeDtypeStruct((SLICES, MINE, BLOCK, LANES), jnp.bfloat16),
        scratch_shapes=[pltpu.VMEM((MINE * PACK, BLOCK, LANE), jnp.float32)],
    )(parts)


def align_kernel(cluster_ref, weight_ref, core_ref, own_ref, got_ref, w_ref, o_ref, acc_ref):
    acc_ref[...] = jnp.zeros_like(acc_ref)
    core = core_ref[0]

    def step(g, carry):
        for half, ref in ((core, own_ref), (1 - core, got_ref)):
            packed = ref[g]
            turned = []
            for i in range(PACK):
                p = (half * GROUPS + g) * PACK + i
                part = jnp.dot(packed[:, i * BLOCK:(i + 1) * BLOCK], w_ref[p], preferred_element_type=jnp.float32)
                turned.append((part * weight_ref[flip(p)]).astype(jnp.bfloat16).astype(jnp.float32))
            for i in range(PACK):
                k = cluster_ref[flip((half * GROUPS + g) * PACK + i)]
                acc_ref[k] = acc_ref[k] + turned[i]
        return carry

    lax.fori_loop(0, GROUPS, step, 0, unroll=4)
    rows = BLOCK // 4

    def put(k, carry):
        for h in range(2):
            pieces = quarters([acc_ref[k, q * rows:(q + 1) * rows, h * LANE:(h + 1) * LANE] for q in range(4)])
            for t in range(4):
                o_ref[4 * h + t, k] = pieces[t].astype(o_ref.dtype)
        return carry

    lax.fori_loop(0, CLUSTERS, put, 0, unroll=2)


def align(cluster_ids, weight, core, own, got, columns):
    return pl.pallas_call(
        align_kernel,
        compiler_params=SMALL,
        in_specs=[SMEM, SMEM, SMEM, VMEM, VMEM, VMEM],
        out_specs=VMEM,
        out_shape=jax.ShapeDtypeStruct((NX * NC, CLUSTERS, BLOCK // 4, LANE), jnp.bfloat16),
        scratch_shapes=[pltpu.VMEM((CLUSTERS, BLOCK, COLS), jnp.float32)],
    )(cluster_ids, weight, core, own, got, columns)


def final_kernel(m_ref, o_ref):
    for zb in range(NZB):
        for a in range(4):
            pieces = quarters([m_ref[0, b % 2, a, zb, b // 2] for b in range(4)])
            o_ref[0, zb * BLOCK:(zb + 1) * BLOCK, a * LANE:(a + 1) * LANE] = jnp.concatenate(pieces, 0)


def final(merged):
    rows = NZB * BLOCK
    return pl.pallas_call(
        final_kernel,
        compiler_params=SMALL,
        grid=(NX,),
        in_specs=[pl.BlockSpec((1,) + merged.shape[1:], lambda x: (x,) + (0,) * 6)],
        out_specs=pl.BlockSpec((1, rows, NC * COLS), lambda x: (0, x, 0)),
        out_shape=jax.ShapeDtypeStruct((1, NX * rows, NC * COLS), merged.dtype),
    )(merged)


def exchange(value, axes):
    return lax.all_to_all(value, axes, split_axis=0, concat_axis=0, tiled=True)


def on_device(w_up, cluster, counts):
    cluster_ids = cluster[:, 0]
    index = jnp.arange(EXPERTS, dtype=jnp.int32)
    labels = jnp.arange(CLUSTERS, dtype=jnp.int32)
    member = cluster_ids[None, :] == labels[:, None]
    score = counts * EXPERTS + (EXPERTS - 1 - index)
    best = jnp.max(jnp.where(member, score[None, :], -1), axis=1)
    leader = EXPERTS - 1 - best % EXPERTS
    anchor_of = jnp.sum(jnp.where(member, leader[:, None], 0), axis=0)
    total = jnp.sum(jnp.where(member, counts[None, :], 0), axis=1).astype(jnp.float32)
    weight = counts.astype(jnp.float32) / jnp.sum(jnp.where(member, total[:, None], 0.0), axis=0)
    core = lax.axis_index("core").astype(jnp.int32).reshape(1)

    held, send = spread(core, w_up)
    rows = join(core, lax.ppermute(send, "core", SWAP), held)
    rows = rows.reshape(NZB * SLICES, -1, COLS)
    rows, anchor_of, weight = lax.optimization_barrier((rows, anchor_of, weight))
    columns = exchange(rows, ("zb", "y", "zc")).reshape(EXPERTS, BLOCK, COLS)

    got = lax.ppermute(grams(anchor_of, core, columns, True), "core", SWAP)
    partial = grams(anchor_of, core, columns, False) + got
    parts = exchange(partial, ("y", "zc"))
    copies = polars(parts.reshape(SLICES, MINE, BLOCK, LANES))
    own = exchange(copies, ("y", "zc")).reshape(GROUPS, BLOCK, LANES)
    merged = align(cluster_ids, weight, core, own, lax.ppermute(own, "core", SWAP), columns)

    merged = exchange(merged.reshape(-1, BLOCK // 4, LANE), ("x", "core", "y", "zb", "zc"))
    return final(merged.reshape(NX, NC, NY, NZB, NZC, BLOCK // 4, LANE))


def solution(mesh):
    grid = Mesh(mesh.devices.reshape(NY, NZB, NZC, NX, NC), ("y", "zb", "zc", "x", "core"))
    return jax.shard_map(
        on_device,
        mesh=grid,
        in_specs=(P(("y", "zb", "zc"), ("x", "core"), None), P(), P()),
        out_specs=P(("y", "zb", "zc"), None, ("x", "core")),
        check_vma=False,
    )
```

```python
import jax
import jax.numpy as jnp
from jax import lax
from jax.experimental import pallas as pl
from jax.experimental.pallas import tpu as pltpu
from jax.sharding import Mesh, PartitionSpec as P

BLOCK = 96
NS_STEPS = 8
NY, NZB, NZC, NX, NC = 4, 4, 2, 4, 2
EXPERTS = 128
CLUSTERS = 32
COLS = 256
PACK = 4
LANE = 128
LANES = PACK * BLOCK
SLICES = NY * NZC
SCALE = 8192.0
GROUPS = EXPERTS // PACK // NC
MINE = GROUPS // SLICES
SWAP = [(0, 1), (1, 0)]
VMEM = pl.BlockSpec(memory_space=pltpu.VMEM)
SMEM = pl.BlockSpec(memory_space=pltpu.SMEM)
ANY = pl.BlockSpec(memory_space=pl.ANY)
NT = (((1,), (1,)), ((), ()))
SMALL = pltpu.CompilerParams(vmem_limit_bytes=20 * 2**20)


def flip(position):
    return ((position >> 3) & 3) * 32 + (position >> 5) * 8 + (position & 7)


def halves(first, second):
    low = lax.broadcasted_iota(jnp.int32, first.shape, 1) < LANE // 2
    return (
        jnp.where(low, first, pltpu.roll(second, LANE // 2, 1)),
        jnp.where(low, pltpu.roll(first, LANE // 2, 1), second),
    )


def spread(core, w, other):
    experts, units, width = w.shape
    blocks = units // BLOCK
    span = width // NX

    def kernel(core_ref, w_ref, o_ref):
        half = 1 - core_ref[0] if other else core_ref[0]
        base = 0 if other else half * blocks
        for e in range(experts):
            for j in range(blocks):
                rows = slice(j * BLOCK, (j + 1) * BLOCK)
                for h in range(NX // 2):
                    for a in range(SLICES // 2):
                        starts = [(2 * h + t) * span + half * (span // NC) + a * LANE for t in range(2)]
                        pair = halves(*[w_ref[e, rows, pl.ds(pl.multiple_of(s, LANE), LANE)] for s in starts])
                        for b in range(2):
                            o_ref[base + j, 2 * a + b, e, :, h * LANE:(h + 1) * LANE] = pair[b]

    shape = (blocks if other else NC * blocks, SLICES, experts, BLOCK, COLS)
    return pl.pallas_call(
        kernel,
        compiler_params=SMALL,
        in_specs=[SMEM, VMEM],
        out_specs=VMEM,
        out_shape=jax.ShapeDtypeStruct(shape, w.dtype),
    )(core, w)


def join_kernel(core_ref, got_ref, held_ref, o_ref, sem):
    blocks = got_ref.shape[0]
    copy = pltpu.make_async_copy(got_ref, o_ref.at[pl.ds((1 - core_ref[0]) * blocks, blocks)], sem)
    copy.start()
    copy.wait()


def join(core, got, held):
    return pl.pallas_call(
        join_kernel,
        compiler_params=SMALL,
        in_specs=[SMEM, ANY, ANY],
        out_specs=ANY,
        out_shape=jax.ShapeDtypeStruct(held.shape, held.dtype),
        scratch_shapes=[pltpu.SemaphoreType.DMA],
        input_output_aliases={2: 0},
    )(core, got, held)


def grams(anchor_of, core, columns, other):
    def kernel(anchor_ref, core_ref, w_ref, o_ref):
        half = 1 - core_ref[0] if other else core_ref[0]

        def step(g, carry):
            parts = []
            for i in range(PACK):
                p = (half * GROUPS + g) * PACK + i
                lead = flip(anchor_ref[flip(p)])
                parts.append(lax.dot_general(w_ref[lead], w_ref[p], NT, preferred_element_type=jnp.float32))
            o_ref[g] = jnp.concatenate(parts, axis=1)
            return carry

        lax.fori_loop(0, GROUPS, step, 0, unroll=4)

    return pl.pallas_call(
        kernel,
        compiler_params=SMALL,
        in_specs=[SMEM, SMEM, VMEM],
        out_specs=VMEM,
        out_shape=jax.ShapeDtypeStruct((GROUPS, BLOCK, LANES), jnp.float32),
    )(anchor_of, core, columns)


def split(value):
    high = value.astype(jnp.bfloat16)
    return high, (value - high.astype(jnp.float32)).astype(jnp.bfloat16)


def fold(product):
    return product[:BLOCK, :LANE] + product[BLOCK:, :LANE] + product[:BLOCK, LANE:]


def polar_kernel(part_ref, o_ref, x_ref):
    count = MINE * PACK
    for g in range(MINE):
        total = part_ref[0, g]
        for s in range(1, SLICES):
            total = total + part_ref[s, g]
        total = total * (1.0 / SCALE)
        for i in range(PACK):
            gram = total[:, i * BLOCK:(i + 1) * BLOCK]
            gram = jnp.concatenate([gram, jnp.zeros((BLOCK, LANE - BLOCK), jnp.float32)], axis=1)
            norm = jnp.sqrt(jnp.sum(jnp.sum(gram * gram, axis=1, keepdims=True), axis=0, keepdims=True) + 1e-06)
            x_ref[g * PACK + i] = gram / norm
    pad = jnp.zeros((LANE - BLOCK, LANE), jnp.bfloat16)

    def square(high, low):
        return lax.dot_general(
            jnp.concatenate([high, low], 0), jnp.concatenate([high, pad, low, pad], 0), NT,
            preferred_element_type=jnp.float32,
        )

    def times(one, two):
        wide = jnp.concatenate([jnp.concatenate([part, pad], 0) for part in two], 1)
        return jnp.dot(jnp.concatenate(one, 0), wide, preferred_element_type=jnp.float32)

    def step(it, carry):
        values = [x_ref[n] for n in range(count)]
        halves = [split(v) for v in values]
        squares = [split(fold(square(*v))) for v in halves]
        cubes = [times(s, v) for s, v in zip(squares, halves)]
        for n in range(count):
            x_ref[n] = 1.5 * values[n] - 0.5 * fold(cubes[n])
        return carry

    lax.fori_loop(0, NS_STEPS, step, 0)
    for g in range(MINE):
        packed = jnp.concatenate([x_ref[g * PACK + i][:, :BLOCK] for i in range(PACK)], axis=1).astype(o_ref.dtype)
        for s in range(SLICES):
            o_ref[s, g] = packed


def polars(parts):
    return pl.pallas_call(
        polar_kernel,
        compiler_params=SMALL,
        in_specs=[VMEM],
        out_specs=VMEM,
        out_shape=jax.ShapeDtypeStruct((SLICES, MINE, BLOCK, LANES), jnp.bfloat16),
        scratch_shapes=[pltpu.VMEM((MINE * PACK, BLOCK, LANE), jnp.float32)],
    )(parts)


def align_kernel(cluster_ref, weight_ref, core_ref, own_ref, got_ref, w_ref, o_ref, acc_ref):
    acc_ref[...] = jnp.zeros_like(acc_ref)
    core = core_ref[0]

    def step(g, carry):
        for half, ref in ((core, own_ref), (1 - core, got_ref)):
            packed = ref[g]
            turned = []
            for i in range(PACK):
                p = (half * GROUPS + g) * PACK + i
                part = jnp.dot(packed[:, i * BLOCK:(i + 1) * BLOCK], w_ref[p], preferred_element_type=jnp.float32)
                turned.append((part * weight_ref[flip(p)]).astype(jnp.bfloat16).astype(jnp.float32))
            for i in range(PACK):
                k = cluster_ref[flip((half * GROUPS + g) * PACK + i)]
                acc_ref[k] = acc_ref[k] + turned[i]
        return carry

    lax.fori_loop(0, GROUPS, step, 0, unroll=4)
    rows = BLOCK // 2

    def put(k, carry):
        for h in range(NX // 2):
            pair = halves(*[acc_ref[k, r * rows:(r + 1) * rows, h * LANE:(h + 1) * LANE] for r in range(2)])
            for t in range(2):
                o_ref[2 * h + t, k] = pair[t].astype(o_ref.dtype)
        return carry

    lax.fori_loop(0, CLUSTERS, put, 0, unroll=2)


def align(cluster_ids, weight, core, own, got, columns):
    return pl.pallas_call(
        align_kernel,
        compiler_params=SMALL,
        in_specs=[SMEM, SMEM, SMEM, VMEM, VMEM, VMEM],
        out_specs=VMEM,
        out_shape=jax.ShapeDtypeStruct((NX, CLUSTERS, BLOCK // 2, LANE), jnp.bfloat16),
        scratch_shapes=[pltpu.VMEM((CLUSTERS, BLOCK, COLS), jnp.float32)],
    )(cluster_ids, weight, core, own, got, columns)


def final_kernel(m_ref, o_ref, buf_ref, sem):
    rows = NZB * BLOCK

    def put(x):
        return pltpu.make_async_copy(buf_ref.at[x % 2], o_ref.at[0, pl.ds(x * rows, rows)], sem.at[x % 2])

    for x in range(NX):
        if x >= 2:
            put(x - 2).wait()
        for zb in range(NZB):
            for y in range(NY):
                pair = halves(m_ref[x, y, zb, 0], m_ref[x, y, zb, 1])
                buf_ref[x % 2, zb * BLOCK:(zb + 1) * BLOCK, y * LANE:(y + 1) * LANE] = jnp.concatenate(pair, 0)
        put(x).start()
    for x in range(NX - 2, NX):
        put(x).wait()


def final(merged):
    rows = NZB * BLOCK
    width = NC * COLS
    return pl.pallas_call(
        final_kernel,
        compiler_params=SMALL,
        in_specs=[VMEM],
        out_specs=ANY,
        out_shape=jax.ShapeDtypeStruct((1, NX * rows, width), merged.dtype),
        scratch_shapes=[pltpu.VMEM((2, rows, width), merged.dtype), pltpu.SemaphoreType.DMA((2,))],
    )(merged)


def exchange(value, axes):
    return lax.all_to_all(value, axes, split_axis=0, concat_axis=0, tiled=True)


def on_device(w_up, cluster, counts):
    cluster_ids = cluster[:, 0]
    index = jnp.arange(EXPERTS, dtype=jnp.int32)
    labels = jnp.arange(CLUSTERS, dtype=jnp.int32)
    member = cluster_ids[None, :] == labels[:, None]
    score = counts * EXPERTS + (EXPERTS - 1 - index)
    best = jnp.max(jnp.where(member, score[None, :], -1), axis=1)
    leader = EXPERTS - 1 - best % EXPERTS
    anchor_of = jnp.sum(jnp.where(member, leader[:, None], 0), axis=0)
    total = jnp.sum(jnp.where(member, counts[None, :], 0), axis=1).astype(jnp.float32)
    weight = counts.astype(jnp.float32) / jnp.sum(jnp.where(member, total[:, None], 0.0), axis=0)
    core = lax.axis_index("core").astype(jnp.int32).reshape(1)

    got = lax.ppermute(spread(core, w_up, True), "core", SWAP)
    rows = join(core, got, spread(core, w_up, False))
    rows = rows.reshape(NZB * SLICES, -1, COLS)
    rows, anchor_of, weight = lax.optimization_barrier((rows, anchor_of, weight))
    columns = exchange(rows, ("zb", "y", "zc")).reshape(EXPERTS, BLOCK, COLS)

    got = lax.ppermute(grams(anchor_of, core, columns, True), "core", SWAP)
    partial = ((grams(anchor_of, core, columns, False) + got) * SCALE).astype(jnp.float16)
    parts = exchange(partial, ("y", "zc")).astype(jnp.float32)
    copies = polars(parts.reshape(SLICES, MINE, BLOCK, LANES))
    own = exchange(copies, ("y", "zc")).reshape(GROUPS, BLOCK, LANES)
    merged = align(cluster_ids, weight, core, own, lax.ppermute(own, "core", SWAP), columns)

    merged = exchange(merged.reshape(-1, BLOCK // 2, LANE), ("x", "y", "zb", "zc"))
    return final(merged.reshape(NX, NY, NZB, NZC, BLOCK // 2, LANE))


def solution(mesh):
    grid = Mesh(mesh.devices.reshape(NY, NZB, NZC, NX, NC), ("y", "zb", "zc", "x", "core"))
    return jax.shard_map(
        on_device,
        mesh=grid,
        in_specs=(P(("y", "zb", "zc"), ("x", "core"), None), P(), P()),
        out_specs=P(("y", "zb", "zc"), None, ("x", "core")),
        check_vma=False,
    )
```

```python
import jax
import jax.numpy as jnp
from jax import lax
from jax.experimental import pallas as pl
from jax.experimental.pallas import tpu as pltpu
from jax.sharding import Mesh, PartitionSpec as P

BLOCK = 96
NS_STEPS = 8
NY, NZB, NZC, NX, NC = 4, 4, 2, 4, 2
EXPERTS = 128
CLUSTERS = 32
COLS = 256
PACK = 4
LANE = 128
LANES = PACK * BLOCK
SLICES = NY * NZC
SCALE = 8192.0
PIECES = 2
GROUPS = EXPERTS // PACK // NC
MINE = GROUPS // SLICES
SWAP = [(0, 1), (1, 0)]
VMEM = pl.BlockSpec(memory_space=pltpu.VMEM)
SMEM = pl.BlockSpec(memory_space=pltpu.SMEM)
ANY = pl.BlockSpec(memory_space=pl.ANY)
NT = (((1,), (1,)), ((), ()))
MEDIUM = pltpu.CompilerParams(vmem_limit_bytes=46 * 2**20)
LARGE = pltpu.CompilerParams(vmem_limit_bytes=58 * 2**20)
SMALL = pltpu.CompilerParams(vmem_limit_bytes=20 * 2**20)


def flip(position):
    return ((position >> 3) & 3) * 32 + (position >> 5) * 8 + (position & 7)


def halves(first, second):
    low = lax.broadcasted_iota(jnp.int32, first.shape, 1) < LANE // 2
    return (
        jnp.where(low, first, pltpu.roll(second, LANE // 2, 1)),
        jnp.where(low, pltpu.roll(first, LANE // 2, 1), second),
    )


def spread(core, w, other, first, count):
    experts, units, width = w.shape
    blocks = units // BLOCK
    span = width // NX
    wide = span // NC

    def kernel(core_ref, w_ref, o_ref, buf_ref, sem):
        half = 1 - core_ref[0] if other else core_ref[0]
        base = 0 if other else half * blocks
        start = pl.multiple_of(half * wide, wide)

        def fetch(e, x):
            source = w_ref.at[first + e, :, pl.ds(x * span + start, wide)]
            return pltpu.make_async_copy(source, buf_ref.at[e, x], sem.at[e, x])

        for e in range(count):
            for x in range(NX):
                fetch(e, x).start()
        for e in range(count):
            for h in range(NX // 2):
                for t in range(2):
                    fetch(e, 2 * h + t).wait()
                for j in range(blocks):
                    rows = slice(j * BLOCK, (j + 1) * BLOCK)
                    for a in range(SLICES // 2):
                        lanes = slice(a * LANE, (a + 1) * LANE)
                        pair = halves(*[buf_ref[e, 2 * h + t, rows, lanes] for t in range(2)])
                        for b in range(2):
                            o_ref[base + j, 2 * a + b, e, :, h * LANE:(h + 1) * LANE] = pair[b]

    shape = (blocks if other else NC * blocks, SLICES, count, BLOCK, COLS)
    return pl.pallas_call(
        kernel,
        compiler_params=LARGE if other else MEDIUM,
        in_specs=[SMEM, pl.BlockSpec(memory_space=pltpu.HBM)],
        out_specs=VMEM,
        out_shape=jax.ShapeDtypeStruct(shape, w.dtype),
        scratch_shapes=[pltpu.VMEM((count, NX, units, wide), w.dtype), pltpu.SemaphoreType.DMA((count, NX))],
    )(core, w)


def join_kernel(core_ref, *refs):
    got_refs, (_, o_ref, sem) = refs[:PIECES], refs[PIECES:]
    blocks, _, count = got_refs[0].shape[:3]
    copies = []
    for k, got_ref in enumerate(got_refs):
        target = o_ref.at[pl.ds((1 - core_ref[0]) * blocks, blocks), :, pl.ds(k * count, count)]
        copies.append(pltpu.make_async_copy(got_ref, target, sem.at[k]))
    for copy in copies:
        copy.start()
    for copy in copies:
        copy.wait()


def join(core, got, held):
    return pl.pallas_call(
        join_kernel,
        compiler_params=SMALL,
        in_specs=[SMEM] + [ANY] * (PIECES + 1),
        out_specs=ANY,
        out_shape=jax.ShapeDtypeStruct(held.shape, held.dtype),
        scratch_shapes=[pltpu.SemaphoreType.DMA((PIECES,))],
        input_output_aliases={1 + PIECES: 0},
    )(core, *got, held)


def grams(anchor_of, core, columns, other):
    def kernel(anchor_ref, core_ref, w_ref, o_ref):
        half = 1 - core_ref[0] if other else core_ref[0]

        def step(g, carry):
            parts = []
            for i in range(PACK):
                p = (half * GROUPS + g) * PACK + i
                lead = flip(anchor_ref[flip(p)])
                parts.append(lax.dot_general(w_ref[lead], w_ref[p], NT, preferred_element_type=jnp.float32))
            o_ref[g] = jnp.concatenate(parts, axis=1)
            return carry

        lax.fori_loop(0, GROUPS, step, 0, unroll=4)

    return pl.pallas_call(
        kernel,
        compiler_params=SMALL,
        in_specs=[SMEM, SMEM, VMEM],
        out_specs=VMEM,
        out_shape=jax.ShapeDtypeStruct((GROUPS, BLOCK, LANES), jnp.float32),
    )(anchor_of, core, columns)


def split(value):
    high = value.astype(jnp.bfloat16)
    return high, (value - high.astype(jnp.float32)).astype(jnp.bfloat16)


def fold(product):
    return product[:BLOCK, :LANE] + product[BLOCK:, :LANE] + product[:BLOCK, LANE:]


def polar_kernel(part_ref, o_ref, x_ref):
    count = MINE * PACK
    for g in range(MINE):
        total = part_ref[0, g]
        for s in range(1, SLICES):
            total = total + part_ref[s, g]
        total = total * (1.0 / SCALE)
        for i in range(PACK):
            gram = total[:, i * BLOCK:(i + 1) * BLOCK]
            gram = jnp.concatenate([gram, jnp.zeros((BLOCK, LANE - BLOCK), jnp.float32)], axis=1)
            norm = jnp.sqrt(jnp.sum(jnp.sum(gram * gram, axis=1, keepdims=True), axis=0, keepdims=True) + 1e-06)
            x_ref[g * PACK + i] = gram / norm
    pad = jnp.zeros((LANE - BLOCK, LANE), jnp.bfloat16)

    def square(high, low):
        return lax.dot_general(
            jnp.concatenate([high, low], 0), jnp.concatenate([high, pad, low, pad], 0), NT,
            preferred_element_type=jnp.float32,
        )

    def times(one, two):
        wide = jnp.concatenate([jnp.concatenate([part, pad], 0) for part in two], 1)
        return jnp.dot(jnp.concatenate(one, 0), wide, preferred_element_type=jnp.float32)

    def step(it, carry):
        values = [x_ref[n] for n in range(count)]
        halves = [split(v) for v in values]
        squares = [split(fold(square(*v))) for v in halves]
        cubes = [times(s, v) for s, v in zip(squares, halves)]
        for n in range(count):
            x_ref[n] = 1.5 * values[n] - 0.5 * fold(cubes[n])
        return carry

    lax.fori_loop(0, NS_STEPS, step, 0)
    for g in range(MINE):
        packed = jnp.concatenate([x_ref[g * PACK + i][:, :BLOCK] for i in range(PACK)], axis=1).astype(o_ref.dtype)
        for s in range(SLICES):
            o_ref[s, g] = packed


def polars(parts):
    return pl.pallas_call(
        polar_kernel,
        compiler_params=SMALL,
        in_specs=[VMEM],
        out_specs=VMEM,
        out_shape=jax.ShapeDtypeStruct((SLICES, MINE, BLOCK, LANES), jnp.bfloat16),
        scratch_shapes=[pltpu.VMEM((MINE * PACK, BLOCK, LANE), jnp.float32)],
    )(parts)


def turn(cluster_ref, weight_ref, polar_ref, w_ref, acc_ref, half):
    def step(g, carry):
        packed = polar_ref[g]
        turned = []
        for i in range(PACK):
            p = (half * GROUPS + g) * PACK + i
            part = jnp.dot(packed[:, i * BLOCK:(i + 1) * BLOCK], w_ref[p], preferred_element_type=jnp.float32)
            turned.append((part * weight_ref[flip(p)]).astype(jnp.bfloat16).astype(jnp.float32))
        for i in range(PACK):
            k = cluster_ref[flip((half * GROUPS + g) * PACK + i)]
            acc_ref[k] = acc_ref[k] + turned[i]
        return carry

    lax.fori_loop(0, GROUPS, step, 0, unroll=8)


def align_own_kernel(cluster_ref, weight_ref, core_ref, own_ref, w_ref, acc_ref):
    acc_ref[...] = jnp.zeros_like(acc_ref)
    turn(cluster_ref, weight_ref, own_ref, w_ref, acc_ref, core_ref[0])


def align_own(cluster_ids, weight, core, own, columns):
    return pl.pallas_call(
        align_own_kernel,
        compiler_params=SMALL,
        in_specs=[SMEM, SMEM, SMEM, VMEM, VMEM],
        out_specs=VMEM,
        out_shape=jax.ShapeDtypeStruct((CLUSTERS, BLOCK, COLS), jnp.float32),
    )(cluster_ids, weight, core, own, columns)


def align_got_kernel(cluster_ref, weight_ref, core_ref, got_ref, w_ref, sum_ref, o_ref, acc_ref):
    acc_ref[...] = sum_ref[...]
    turn(cluster_ref, weight_ref, got_ref, w_ref, acc_ref, 1 - core_ref[0])
    rows = BLOCK // 2

    def put(k, carry):
        for h in range(NX // 2):
            pair = halves(*[acc_ref[k, r * rows:(r + 1) * rows, h * LANE:(h + 1) * LANE] for r in range(2)])
            for t in range(2):
                o_ref[2 * h + t, k] = pair[t].astype(o_ref.dtype)
        return carry

    lax.fori_loop(0, CLUSTERS, put, 0, unroll=2)


def align_got(cluster_ids, weight, core, got, columns, sums):
    return pl.pallas_call(
        align_got_kernel,
        compiler_params=SMALL,
        in_specs=[SMEM, SMEM, SMEM, VMEM, VMEM, VMEM],
        out_specs=VMEM,
        out_shape=jax.ShapeDtypeStruct((NX, CLUSTERS, BLOCK // 2, LANE), jnp.bfloat16),
        scratch_shapes=[pltpu.VMEM((CLUSTERS, BLOCK, COLS), jnp.float32)],
    )(cluster_ids, weight, core, got, columns, sums)


def final_kernel(m_ref, o_ref, buf_ref, sem):
    rows = NZB * BLOCK

    def put(x):
        return pltpu.make_async_copy(buf_ref.at[x % 2], o_ref.at[0, pl.ds(x * rows, rows)], sem.at[x % 2])

    for x in range(NX):
        if x >= 2:
            put(x - 2).wait()
        for zb in range(NZB):
            for y in range(NY):
                pair = halves(m_ref[x, y, zb, 0], m_ref[x, y, zb, 1])
                buf_ref[x % 2, zb * BLOCK:(zb + 1) * BLOCK, y * LANE:(y + 1) * LANE] = jnp.concatenate(pair, 0)
        put(x).start()
    for x in range(NX - 2, NX):
        put(x).wait()


def final(merged):
    rows = NZB * BLOCK
    width = NC * COLS
    return pl.pallas_call(
        final_kernel,
        compiler_params=SMALL,
        in_specs=[VMEM],
        out_specs=ANY,
        out_shape=jax.ShapeDtypeStruct((1, NX * rows, width), merged.dtype),
        scratch_shapes=[pltpu.VMEM((2, rows, width), merged.dtype), pltpu.SemaphoreType.DMA((2,))],
    )(merged)


def exchange(value, axes):
    return lax.all_to_all(value, axes, split_axis=0, concat_axis=0, tiled=True)


def on_device(w_up, cluster, counts):
    cluster_ids = cluster[:, 0]
    index = jnp.arange(EXPERTS, dtype=jnp.int32)
    labels = jnp.arange(CLUSTERS, dtype=jnp.int32)
    member = cluster_ids[None, :] == labels[:, None]
    score = counts * EXPERTS + (EXPERTS - 1 - index)
    best = jnp.max(jnp.where(member, score[None, :], -1), axis=1)
    leader = EXPERTS - 1 - best % EXPERTS
    anchor_of = jnp.sum(jnp.where(member, leader[:, None], 0), axis=0)
    total = jnp.sum(jnp.where(member, counts[None, :], 0), axis=1).astype(jnp.float32)
    weight = counts.astype(jnp.float32) / jnp.sum(jnp.where(member, total[:, None], 0.0), axis=0)
    core = lax.axis_index("core").astype(jnp.int32).reshape(1)

    experts = w_up.shape[0]
    count = experts // PIECES
    sent = [spread(core, w_up, True, k * count, count) for k in range(PIECES)]
    got = [lax.ppermute(piece, "core", SWAP) for piece in sent]
    rows = join(core, got, spread(core, w_up, False, 0, experts))
    rows = rows.reshape(NZB * SLICES, -1, COLS)
    rows, anchor_of, weight = lax.optimization_barrier((rows, anchor_of, weight))
    columns = exchange(rows, ("zb", "y", "zc")).reshape(EXPERTS, BLOCK, COLS)

    got = lax.ppermute(grams(anchor_of, core, columns, True), "core", SWAP)
    partial = ((grams(anchor_of, core, columns, False) + got) * SCALE).astype(jnp.float16)
    parts = exchange(partial, ("y", "zc")).astype(jnp.float32)
    copies = polars(parts.reshape(SLICES, MINE, BLOCK, LANES))
    own = exchange(copies, ("y", "zc")).reshape(GROUPS, BLOCK, LANES)
    got = lax.ppermute(own, "core", SWAP)
    merged = align_got(cluster_ids, weight, core, got, columns, align_own(cluster_ids, weight, core, own, columns))

    merged = exchange(merged.reshape(-1, BLOCK // 2, LANE), ("x", "y", "zb", "zc"))
    return final(merged.reshape(NX, NY, NZB, NZC, BLOCK // 2, LANE))


def solution(mesh):
    grid = Mesh(mesh.devices.reshape(NY, NZB, NZC, NX, NC), ("y", "zb", "zc", "x", "core"))
    return jax.shard_map(
        on_device,
        mesh=grid,
        in_specs=(P(("y", "zb", "zc"), ("x", "core"), None), P(), P()),
        out_specs=P(("y", "zb", "zc"), None, ("x", "core")),
        check_vma=False,
    )
```

```python
import functools

import jax
import jax.numpy as jnp
from jax import lax
from jax.experimental import pallas as pl
from jax.experimental.pallas import tpu as pltpu
from jax.sharding import Mesh, PartitionSpec as P


BLOCK = 96
NS_STEPS = 8
NY, NZB, NZC, NX, NC = 4, 4, 2, 4, 2
EXPERTS = 128
CLUSTERS = 32
COLS = 256
PACK = 4
LANE = 128
LANES = PACK * BLOCK
SLICES = NY * NZC
SCALE = 8192.0
PARTS = 2
ROWS = BLOCK // PARTS
GROUPS = EXPERTS // PACK // NC
MINE = GROUPS // SLICES
SWAP = [(0, 1), (1, 0)]
VMEM = pl.BlockSpec(memory_space=pltpu.VMEM)
SMEM = pl.BlockSpec(memory_space=pltpu.SMEM)
ANY = pl.BlockSpec(memory_space=pl.ANY)
NT = (((1,), (1,)), ((), ()))
SMALL = pltpu.CompilerParams(vmem_limit_bytes=20 * 2**20)


def flip(position):
    return ((position >> 3) & 3) * 32 + (position >> 5) * 8 + (position & 7)


def halves(first, second):
    low = lax.broadcasted_iota(jnp.int32, first.shape, 1) < LANE // 2
    return (
        jnp.where(low, first, pltpu.roll(second, LANE // 2, 1)),
        jnp.where(low, pltpu.roll(first, LANE // 2, 1), second),
    )


def spread(core, w, other):
    experts, units, width = w.shape
    blocks = units // BLOCK
    span = width // NX

    def kernel(core_ref, w_ref, o_ref):
        half = 1 - core_ref[0] if other else core_ref[0]
        base = 0 if other else half * blocks
        for e in range(experts):
            for j in range(blocks):
                rows = slice(j * BLOCK, (j + 1) * BLOCK)
                for h in range(NX // 2):
                    for a in range(SLICES // 2):
                        starts = [(2 * h + t) * span + half * (span // NC) + a * LANE for t in range(2)]
                        pair = halves(*[w_ref[e, rows, pl.ds(pl.multiple_of(s, LANE), LANE)] for s in starts])
                        for b in range(2):
                            o_ref[base + j, 2 * a + b, e, :, h * LANE:(h + 1) * LANE] = pair[b]

    shape = (blocks if other else NC * blocks, SLICES, experts, BLOCK, COLS)
    return pl.pallas_call(
        kernel,
        compiler_params=SMALL,
        in_specs=[SMEM, VMEM],
        out_specs=VMEM,
        out_shape=jax.ShapeDtypeStruct(shape, w.dtype),
    )(core, w)


def join_kernel(core_ref, got_ref, held_ref, o_ref, sem):
    blocks = got_ref.shape[0]
    copy = pltpu.make_async_copy(got_ref, o_ref.at[pl.ds((1 - core_ref[0]) * blocks, blocks)], sem)
    copy.start()
    copy.wait()


def join(core, got, held):
    return pl.pallas_call(
        join_kernel,
        compiler_params=SMALL,
        in_specs=[SMEM, ANY, ANY],
        out_specs=ANY,
        out_shape=jax.ShapeDtypeStruct(held.shape, held.dtype),
        scratch_shapes=[pltpu.SemaphoreType.DMA],
        input_output_aliases={2: 0},
    )(core, got, held)


def grams(anchor_of, core, columns, other):
    def kernel(anchor_ref, core_ref, w_ref, o_ref):
        half = 1 - core_ref[0] if other else core_ref[0]

        def step(g, carry):
            parts = []
            for i in range(PACK):
                p = (half * GROUPS + g) * PACK + i
                lead = flip(anchor_ref[flip(p)])
                parts.append(lax.dot_general(w_ref[lead], w_ref[p], NT, preferred_element_type=jnp.float32))
            o_ref[g] = jnp.concatenate(parts, axis=1)
            return carry

        lax.fori_loop(0, GROUPS, step, 0, unroll=4)

    return pl.pallas_call(
        kernel,
        compiler_params=SMALL,
        in_specs=[SMEM, SMEM, VMEM],
        out_specs=VMEM,
        out_shape=jax.ShapeDtypeStruct((GROUPS, BLOCK, LANES), jnp.float32),
    )(anchor_of, core, columns)


def split(value):
    high = value.astype(jnp.bfloat16)
    return high, (value - high.astype(jnp.float32)).astype(jnp.bfloat16)


def fold(product):
    return product[:BLOCK, :LANE] + product[BLOCK:, :LANE] + product[:BLOCK, LANE:]


def polar_kernel(part_ref, *refs):
    o_refs, x_ref = refs[:PARTS], refs[PARTS]
    count = MINE * PACK
    for g in range(MINE):
        total = part_ref[0, g]
        for s in range(1, SLICES):
            total = total + part_ref[s, g]
        total = total * (1.0 / SCALE)
        for i in range(PACK):
            gram = total[:, i * BLOCK:(i + 1) * BLOCK]
            gram = jnp.concatenate([gram, jnp.zeros((BLOCK, LANE - BLOCK), jnp.float32)], axis=1)
            norm = jnp.sqrt(jnp.sum(jnp.sum(gram * gram, axis=1, keepdims=True), axis=0, keepdims=True) + 1e-06)
            x_ref[g * PACK + i] = gram / norm
    pad = jnp.zeros((LANE - BLOCK, LANE), jnp.bfloat16)

    def square(high, low):
        return lax.dot_general(
            jnp.concatenate([high, low], 0), jnp.concatenate([high, pad, low, pad], 0), NT,
            preferred_element_type=jnp.float32,
        )

    def times(one, two):
        wide = jnp.concatenate([jnp.concatenate([part, pad], 0) for part in two], 1)
        return jnp.dot(jnp.concatenate(one, 0), wide, preferred_element_type=jnp.float32)

    def step(it, carry):
        values = [x_ref[n] for n in range(count)]
        halves = [split(v) for v in values]
        squares = [split(fold(square(*v))) for v in halves]
        cubes = [times(s, v) for s, v in zip(squares, halves)]
        for n in range(count):
            x_ref[n] = 1.5 * values[n] - 0.5 * fold(cubes[n])
        return carry

    lax.fori_loop(0, NS_STEPS, step, 0)
    for g in range(MINE):
        packed = jnp.concatenate([x_ref[g * PACK + i][:, :BLOCK] for i in range(PACK)], axis=1).astype(jnp.bfloat16)
        for s in range(SLICES):
            o_refs[0][s, g] = packed[:ROWS]
        o_refs[1][g] = packed[ROWS:]


def polars(parts):
    return pl.pallas_call(
        polar_kernel,
        compiler_params=SMALL,
        in_specs=[VMEM],
        out_specs=[VMEM] * PARTS,
        out_shape=[
            jax.ShapeDtypeStruct((SLICES, MINE, ROWS, LANES), jnp.bfloat16),
            jax.ShapeDtypeStruct((MINE, ROWS, LANES), jnp.bfloat16),
        ],
        scratch_shapes=[pltpu.VMEM((MINE * PACK, BLOCK, LANE), jnp.float32)],
    )(parts)


def align_kernel(cluster_ref, weight_ref, place_ref, own_ref, got_ref, w_ref, o_ref, acc_ref, *, relative):
    acc_ref[...] = jnp.zeros_like(acc_ref)
    core = place_ref[0]

    def step(g, carry):
        held = g
        if relative:
            source = g // MINE
            behind = (place_ref[1] + NY - source // NZC) % NY
            held = (behind * NZC + (place_ref[2] + source) % NZC) * MINE + g % MINE
        for half, ref in ((core, own_ref), (1 - core, got_ref)):
            packed = ref[held]
            turned = []
            for i in range(PACK):
                p = (half * GROUPS + g) * PACK + i
                part = jnp.dot(packed[:, i * BLOCK:(i + 1) * BLOCK], w_ref[p], preferred_element_type=jnp.float32)
                turned.append((part * weight_ref[flip(p)]).astype(jnp.bfloat16).astype(jnp.float32))
            for i in range(PACK):
                k = cluster_ref[flip((half * GROUPS + g) * PACK + i)]
                acc_ref[k] = acc_ref[k] + turned[i]
        return carry

    lax.fori_loop(0, GROUPS, step, 0, unroll=4)
    rows = ROWS // 2

    def put(k, carry):
        for h in range(NX // 2):
            pair = halves(*[acc_ref[k, r * rows:(r + 1) * rows, h * LANE:(h + 1) * LANE] for r in range(2)])
            for t in range(2):
                o_ref[2 * h + t, k] = pair[t].astype(o_ref.dtype)
        return carry

    lax.fori_loop(0, CLUSTERS, put, 0, unroll=2)


def align(cluster_ids, weight, place, own, got, columns, relative):
    return pl.pallas_call(
        functools.partial(align_kernel, relative=relative),
        compiler_params=SMALL,
        in_specs=[SMEM, SMEM, SMEM, VMEM, VMEM, VMEM],
        out_specs=VMEM,
        out_shape=jax.ShapeDtypeStruct((NX, CLUSTERS, ROWS // 2, LANE), jnp.bfloat16),
        scratch_shapes=[pltpu.VMEM((CLUSTERS, ROWS, COLS), jnp.float32)],
    )(cluster_ids, weight, place, own, got, columns)


def final_kernel(*refs):
    m_refs, (o_ref, buf_ref, sem) = refs[:PARTS], refs[PARTS:]
    rows = NZB * BLOCK

    def put(x):
        return pltpu.make_async_copy(buf_ref.at[x % 2], o_ref.at[0, pl.ds(x * rows, rows)], sem.at[x % 2])

    for x in range(NX):
        if x >= 2:
            put(x - 2).wait()
        for zb in range(NZB):
            for y in range(NY):
                pieces = [p for m_ref in m_refs for p in halves(m_ref[x, y, zb, 0], m_ref[x, y, zb, 1])]
                buf_ref[x % 2, zb * BLOCK:(zb + 1) * BLOCK, y * LANE:(y + 1) * LANE] = jnp.concatenate(pieces, 0)
        put(x).start()
    for x in range(NX - 2, NX):
        put(x).wait()


def final(*merged):
    rows = NZB * BLOCK
    width = NC * COLS
    return pl.pallas_call(
        final_kernel,
        compiler_params=SMALL,
        in_specs=[VMEM] * PARTS,
        out_specs=ANY,
        out_shape=jax.ShapeDtypeStruct((1, NX * rows, width), jnp.bfloat16),
        scratch_shapes=[pltpu.VMEM((2, rows, width), jnp.bfloat16), pltpu.SemaphoreType.DMA((2,))],
    )(*merged)


def exchange(value, axes):
    return lax.all_to_all(value, axes, split_axis=0, concat_axis=0, tiled=True)


def on_device(w_up, cluster, counts):
    cluster_ids = cluster[:, 0]
    index = jnp.arange(EXPERTS, dtype=jnp.int32)
    labels = jnp.arange(CLUSTERS, dtype=jnp.int32)
    member = cluster_ids[None, :] == labels[:, None]
    score = counts * EXPERTS + (EXPERTS - 1 - index)
    best = jnp.max(jnp.where(member, score[None, :], -1), axis=1)
    leader = EXPERTS - 1 - best % EXPERTS
    anchor_of = jnp.sum(jnp.where(member, leader[:, None], 0), axis=0)
    total = jnp.sum(jnp.where(member, counts[None, :], 0), axis=1).astype(jnp.float32)
    weight = counts.astype(jnp.float32) / jnp.sum(jnp.where(member, total[:, None], 0.0), axis=0)
    core = lax.axis_index("core").astype(jnp.int32).reshape(1)

    got = lax.ppermute(spread(core, w_up, True), "core", SWAP)
    rows = join(core, got, spread(core, w_up, False))
    rows = rows.reshape(NZB * SLICES, -1, COLS)
    rows, anchor_of, weight = lax.optimization_barrier((rows, anchor_of, weight))
    columns = exchange(rows, ("zb", "y", "zc")).reshape(EXPERTS, BLOCK, COLS)

    got = lax.ppermute(grams(anchor_of, core, columns, True), "core", SWAP)
    partial = ((grams(anchor_of, core, columns, False) + got) * SCALE).astype(jnp.float16)
    parts = exchange(partial, ("y", "zc")).astype(jnp.float32)
    copies = polars(parts.reshape(SLICES, MINE, BLOCK, LANES))

    place = jnp.stack([lax.axis_index(name).astype(jnp.int32) for name in ("core", "y", "zc")])

    def serve(rows):
        rows = exchange(rows.reshape(-1, ROWS // 2, LANE), ("x", "y", "zb", "zc"))
        return rows.reshape(NX, NY, NZB, NZC, ROWS // 2, LANE)

    def ahead(dy, dz):
        return [(y * NZC + z, (y + dy) % NY * NZC + (z + dz) % NZC) for y in range(NY) for z in range(NZC)]

    own = exchange(copies[0], ("y", "zc")).reshape(GROUPS, ROWS, LANES)
    merged = align(cluster_ids, weight, place, own, lax.ppermute(own, "core", SWAP), columns, False)
    first = serve(merged)
    pieces = [copies[1]]
    for offset in range(1, SLICES):
        pieces.append(lax.ppermute(copies[1], ("y", "zc"), ahead(offset // NZC, offset % NZC)))
    own = jnp.concatenate(pieces, axis=0)
    second = serve(align(cluster_ids, weight, place, own, lax.ppermute(own, "core", SWAP), columns, True))
    return final(first, second)


def solution(mesh):
    grid = Mesh(mesh.devices.reshape(NY, NZB, NZC, NX, NC), ("y", "zb", "zc", "x", "core"))
    return jax.shard_map(
        on_device,
        mesh=grid,
        in_specs=(P(("y", "zb", "zc"), ("x", "core"), None), P(), P()),
        out_specs=P(("y", "zb", "zc"), None, ("x", "core")),
        check_vma=False,
    )
```

```python
import jax
import jax.numpy as jnp
from jax import lax
from jax.experimental import pallas as pl
from jax.experimental.pallas import tpu as pltpu
from jax.sharding import Mesh, PartitionSpec as P

BLOCK = 96
NS_STEPS = 8
NY, NZB, NZC, NX, NC = 4, 4, 2, 4, 2
EXPERTS = 128
CLUSTERS = 32
COLS = 256
PACK = 4
LANE = 128
LANES = PACK * BLOCK
SLICES = NY * NZC
SCALE = 8192.0
PIECES = 2
GROUPS = EXPERTS // PACK // NC
MINE = GROUPS // SLICES
SWAP = [(0, 1), (1, 0)]
VMEM = pl.BlockSpec(memory_space=pltpu.VMEM)
SMEM = pl.BlockSpec(memory_space=pltpu.SMEM)
ANY = pl.BlockSpec(memory_space=pl.ANY)
NT = (((1,), (1,)), ((), ()))
MEDIUM = pltpu.CompilerParams(vmem_limit_bytes=46 * 2**20)
LARGE = pltpu.CompilerParams(vmem_limit_bytes=58 * 2**20)
SMALL = pltpu.CompilerParams(vmem_limit_bytes=20 * 2**20)


def flip(position):
    return ((position >> 3) & 3) * 32 + (position >> 5) * 8 + (position & 7)


def halves(first, second):
    low = lax.broadcasted_iota(jnp.int32, first.shape, 1) < LANE // 2
    return (
        jnp.where(low, first, pltpu.roll(second, LANE // 2, 1)),
        jnp.where(low, pltpu.roll(first, LANE // 2, 1), second),
    )


def spread(core, w, other, first, count):
    experts, units, width = w.shape
    blocks = units // BLOCK
    span = width // NX
    wide = span // NC

    def kernel(core_ref, w_ref, o_ref, buf_ref, sem):
        half = 1 - core_ref[0] if other else core_ref[0]
        base = 0 if other else half * blocks
        start = pl.multiple_of(half * wide, wide)

        def fetch(e, x):
            source = w_ref.at[first + e, :, pl.ds(x * span + start, wide)]
            return pltpu.make_async_copy(source, buf_ref.at[e, x], sem.at[e, x])

        for e in range(count):
            for x in range(NX):
                fetch(e, x).start()
        for e in range(count):
            for h in range(NX // 2):
                for t in range(2):
                    fetch(e, 2 * h + t).wait()
                for j in range(blocks):
                    rows = slice(j * BLOCK, (j + 1) * BLOCK)
                    for a in range(SLICES // 2):
                        lanes = slice(a * LANE, (a + 1) * LANE)
                        pair = halves(*[buf_ref[e, 2 * h + t, rows, lanes] for t in range(2)])
                        for b in range(2):
                            o_ref[base + j, 2 * a + b, e, :, h * LANE:(h + 1) * LANE] = pair[b]

    shape = (blocks if other else NC * blocks, SLICES, count, BLOCK, COLS)
    return pl.pallas_call(
        kernel,
        compiler_params=LARGE if other else MEDIUM,
        in_specs=[SMEM, pl.BlockSpec(memory_space=pltpu.HBM)],
        out_specs=VMEM,
        out_shape=jax.ShapeDtypeStruct(shape, w.dtype),
        scratch_shapes=[pltpu.VMEM((count, NX, units, wide), w.dtype), pltpu.SemaphoreType.DMA((count, NX))],
    )(core, w)


def join_kernel(core_ref, *refs):
    got_refs, (_, o_ref, sem) = refs[:PIECES], refs[PIECES:]
    blocks, _, count = got_refs[0].shape[:3]
    copies = []
    for k, got_ref in enumerate(got_refs):
        target = o_ref.at[pl.ds((1 - core_ref[0]) * blocks, blocks), :, pl.ds(k * count, count)]
        copies.append(pltpu.make_async_copy(got_ref, target, sem.at[k]))
    for copy in copies:
        copy.start()
    for copy in copies:
        copy.wait()


def join(core, got, held):
    return pl.pallas_call(
        join_kernel,
        compiler_params=SMALL,
        in_specs=[SMEM] + [ANY] * (PIECES + 1),
        out_specs=ANY,
        out_shape=jax.ShapeDtypeStruct(held.shape, held.dtype),
        scratch_shapes=[pltpu.SemaphoreType.DMA((PIECES,))],
        input_output_aliases={1 + PIECES: 0},
    )(core, *got, held)


def grams(anchor_of, core, columns, other):
    def kernel(anchor_ref, core_ref, w_ref, o_ref):
        half = 1 - core_ref[0] if other else core_ref[0]

        def step(g, carry):
            parts = []
            for i in range(PACK):
                p = (half * GROUPS + g) * PACK + i
                lead = flip(anchor_ref[flip(p)])
                parts.append(lax.dot_general(w_ref[lead], w_ref[p], NT, preferred_element_type=jnp.float32))
            o_ref[g] = jnp.concatenate(parts, axis=1)
            return carry

        lax.fori_loop(0, GROUPS, step, 0, unroll=4)

    return pl.pallas_call(
        kernel,
        compiler_params=SMALL,
        in_specs=[SMEM, SMEM, VMEM],
        out_specs=VMEM,
        out_shape=jax.ShapeDtypeStruct((GROUPS, BLOCK, LANES), jnp.float32),
    )(anchor_of, core, columns)


def split(value):
    high = value.astype(jnp.bfloat16)
    return high, (value - high.astype(jnp.float32)).astype(jnp.bfloat16)


def fold(product):
    return product[:BLOCK, :LANE] + product[BLOCK:, :LANE] + product[:BLOCK, LANE:]


def polar_kernel(part_ref, o_ref, x_ref):
    count = MINE * PACK
    for g in range(MINE):
        total = part_ref[0, g]
        for s in range(1, SLICES):
            total = total + part_ref[s, g]
        total = total * (1.0 / SCALE)
        for i in range(PACK):
            gram = total[:, i * BLOCK:(i + 1) * BLOCK]
            gram = jnp.concatenate([gram, jnp.zeros((BLOCK, LANE - BLOCK), jnp.float32)], axis=1)
            norm = jnp.sqrt(jnp.sum(jnp.sum(gram * gram, axis=1, keepdims=True), axis=0, keepdims=True) + 1e-06)
            x_ref[g * PACK + i] = gram / norm
    pad = jnp.zeros((LANE - BLOCK, LANE), jnp.bfloat16)

    def square(high, low):
        return lax.dot_general(
            jnp.concatenate([high, low], 0), jnp.concatenate([high, pad, low, pad], 0), NT,
            preferred_element_type=jnp.float32,
        )

    def times(one, two):
        wide = jnp.concatenate([jnp.concatenate([part, pad], 0) for part in two], 1)
        return jnp.dot(jnp.concatenate(one, 0), wide, preferred_element_type=jnp.float32)

    def step(it, carry):
        values = [x_ref[n] for n in range(count)]
        halves = [split(v) for v in values]
        squares = [split(fold(square(*v))) for v in halves]
        cubes = [times(s, v) for s, v in zip(squares, halves)]
        for n in range(count):
            x_ref[n] = 1.5 * values[n] - 0.5 * fold(cubes[n])
        return carry

    lax.fori_loop(0, NS_STEPS, step, 0)
    for g in range(MINE):
        packed = jnp.concatenate([x_ref[g * PACK + i][:, :BLOCK] for i in range(PACK)], axis=1).astype(o_ref.dtype)
        for s in range(SLICES):
            o_ref[s, g] = packed


def polars(parts):
    return pl.pallas_call(
        polar_kernel,
        compiler_params=SMALL,
        in_specs=[VMEM],
        out_specs=VMEM,
        out_shape=jax.ShapeDtypeStruct((SLICES, MINE, BLOCK, LANES), jnp.bfloat16),
        scratch_shapes=[pltpu.VMEM((MINE * PACK, BLOCK, LANE), jnp.float32)],
    )(parts)


def turn(cluster_ref, weight_ref, polar_ref, w_ref, acc_ref, half):
    def step(g, carry):
        packed = polar_ref[g]
        turned = []
        for i in range(PACK):
            p = (half * GROUPS + g) * PACK + i
            part = jnp.dot(packed[:, i * BLOCK:(i + 1) * BLOCK], w_ref[p], preferred_element_type=jnp.float32)
            turned.append((part * weight_ref[flip(p)]).astype(jnp.bfloat16).astype(jnp.float32))
        for i in range(PACK):
            k = cluster_ref[flip((half * GROUPS + g) * PACK + i)]
            acc_ref[k] = acc_ref[k] + turned[i]
        return carry

    lax.fori_loop(0, GROUPS, step, 0, unroll=8)


def align_own_kernel(cluster_ref, weight_ref, core_ref, own_ref, w_ref, acc_ref):
    acc_ref[...] = jnp.zeros_like(acc_ref)
    turn(cluster_ref, weight_ref, own_ref, w_ref, acc_ref, core_ref[0])


def align_own(cluster_ids, weight, core, own, columns):
    return pl.pallas_call(
        align_own_kernel,
        compiler_params=SMALL,
        in_specs=[SMEM, SMEM, SMEM, VMEM, VMEM],
        out_specs=VMEM,
        out_shape=jax.ShapeDtypeStruct((CLUSTERS, BLOCK, COLS), jnp.float32),
    )(cluster_ids, weight, core, own, columns)


def align_got_kernel(cluster_ref, weight_ref, core_ref, got_ref, w_ref, sum_ref, o_ref, acc_ref):
    acc_ref[...] = sum_ref[...]
    turn(cluster_ref, weight_ref, got_ref, w_ref, acc_ref, 1 - core_ref[0])
    rows = BLOCK // 2

    def put(k, carry):
        slot = k % (NZB * NZC) * NY + k // (NZB * NZC)
        for h in range(NX // 2):
            pair = halves(*[acc_ref[k, r * rows:(r + 1) * rows, h * LANE:(h + 1) * LANE] for r in range(2)])
            for t in range(2):
                o_ref[slot, 2 * h + t] = pair[t].astype(o_ref.dtype)
        return carry

    lax.fori_loop(0, CLUSTERS, put, 0, unroll=2)


def align_got(cluster_ids, weight, core, got, columns, sums):
    return pl.pallas_call(
        align_got_kernel,
        compiler_params=SMALL,
        in_specs=[SMEM, SMEM, SMEM, VMEM, VMEM, VMEM],
        out_specs=VMEM,
        out_shape=jax.ShapeDtypeStruct((CLUSTERS, NX, BLOCK // 2, LANE), jnp.bfloat16),
        scratch_shapes=[pltpu.VMEM((CLUSTERS, BLOCK, COLS), jnp.float32)],
    )(cluster_ids, weight, core, got, columns, sums)


def final_kernel(m_ref, o_ref, buf_ref, sem):
    rows = NZB * BLOCK

    def put(x):
        return pltpu.make_async_copy(buf_ref.at[x % 2], o_ref.at[0, pl.ds(x * rows, rows)], sem.at[x % 2])

    for x in range(NX):
        if x >= 2:
            put(x - 2).wait()
        for zb in range(NZB):
            for y in range(NY):
                pair = halves(m_ref[zb, 0, y, x], m_ref[zb, 1, y, x])
                buf_ref[x % 2, zb * BLOCK:(zb + 1) * BLOCK, y * LANE:(y + 1) * LANE] = jnp.concatenate(pair, 0)
        put(x).start()
    for x in range(NX - 2, NX):
        put(x).wait()


def final(merged):
    rows = NZB * BLOCK
    width = NC * COLS
    return pl.pallas_call(
        final_kernel,
        compiler_params=SMALL,
        in_specs=[VMEM],
        out_specs=ANY,
        out_shape=jax.ShapeDtypeStruct((1, NX * rows, width), merged.dtype),
        scratch_shapes=[pltpu.VMEM((2, rows, width), merged.dtype), pltpu.SemaphoreType.DMA((2,))],
    )(merged)


def exchange(value, axes):
    return lax.all_to_all(value, axes, split_axis=0, concat_axis=0, tiled=True)


def on_device(w_up, cluster, counts):
    cluster_ids = cluster[:, 0]
    index = jnp.arange(EXPERTS, dtype=jnp.int32)
    labels = jnp.arange(CLUSTERS, dtype=jnp.int32)
    member = cluster_ids[None, :] == labels[:, None]
    score = counts * EXPERTS + (EXPERTS - 1 - index)
    best = jnp.max(jnp.where(member, score[None, :], -1), axis=1)
    leader = EXPERTS - 1 - best % EXPERTS
    anchor_of = jnp.sum(jnp.where(member, leader[:, None], 0), axis=0)
    total = jnp.sum(jnp.where(member, counts[None, :], 0), axis=1).astype(jnp.float32)
    weight = counts.astype(jnp.float32) / jnp.sum(jnp.where(member, total[:, None], 0.0), axis=0)
    core = lax.axis_index("core").astype(jnp.int32).reshape(1)

    experts = w_up.shape[0]
    count = experts // PIECES
    sent = [spread(core, w_up, True, k * count, count) for k in range(PIECES)]
    got = [lax.ppermute(piece, "core", SWAP) for piece in sent]
    rows = join(core, got, spread(core, w_up, False, 0, experts))
    rows = rows.reshape(NZB * SLICES, -1, COLS)
    rows, anchor_of, weight = lax.optimization_barrier((rows, anchor_of, weight))
    columns = exchange(rows, ("zb", "y", "zc")).reshape(EXPERTS, BLOCK, COLS)

    got = lax.ppermute(grams(anchor_of, core, columns, True), "core", SWAP)
    partial = ((grams(anchor_of, core, columns, False) + got) * SCALE).astype(jnp.float16)
    parts = exchange(partial, ("zc", "y")).astype(jnp.float32)
    copies = polars(parts.reshape(SLICES, MINE, BLOCK, LANES))
    own = exchange(copies, ("zc", "y")).reshape(GROUPS, BLOCK, LANES)
    got = lax.ppermute(own, "core", SWAP)
    merged = align_got(cluster_ids, weight, core, got, columns, align_own(cluster_ids, weight, core, own, columns))

    merged = exchange(merged.reshape(-1, BLOCK // 2, LANE), ("zb", "zc", "y", "x"))
    return final(merged.reshape(NZB, NZC, NY, NX, BLOCK // 2, LANE))


def solution(mesh):
    grid = Mesh(mesh.devices.reshape(NY, NZB, NZC, NX, NC), ("y", "zb", "zc", "x", "core"))
    return jax.shard_map(
        on_device,
        mesh=grid,
        in_specs=(P(("y", "zb", "zc"), ("x", "core"), None), P(), P()),
        out_specs=P(("y", "zb", "zc"), None, ("x", "core")),
        check_vma=False,
    )
```

```python
import jax
import jax.numpy as jnp
from jax import lax
from jax.experimental import pallas as pl
from jax.experimental.pallas import tpu as pltpu
from jax.sharding import Mesh, PartitionSpec as P

BLOCK = 96
NS_STEPS = 8
NY, NZB, NZC, NX, NC = 4, 4, 2, 4, 2
EXPERTS = 128
CLUSTERS = 32
COLS = 256
PACK = 4
LANE = 128
LANES = PACK * BLOCK
SLICES = NY * NZC
SCALE = 8192.0
PIECES = 2
GROUPS = EXPERTS // PACK // NC
MINE = GROUPS // SLICES
SWAP = [(0, 1), (1, 0)]
VMEM = pl.BlockSpec(memory_space=pltpu.VMEM)
SMEM = pl.BlockSpec(memory_space=pltpu.SMEM)
ANY = pl.BlockSpec(memory_space=pl.ANY)
NT = (((1,), (1,)), ((), ()))
MEDIUM = pltpu.CompilerParams(vmem_limit_bytes=46 * 2**20)
LARGE = pltpu.CompilerParams(vmem_limit_bytes=58 * 2**20)
SMALL = pltpu.CompilerParams(vmem_limit_bytes=20 * 2**20)


def flip(position):
    return ((position >> 3) & 3) * 32 + (position >> 5) * 8 + (position & 7)


def halves(first, second):
    low = lax.broadcasted_iota(jnp.int32, first.shape, 1) < LANE // 2
    return (
        jnp.where(low, first, pltpu.roll(second, LANE // 2, 1)),
        jnp.where(low, pltpu.roll(first, LANE // 2, 1), second),
    )


def spread(core, w, other, first, count):
    experts, units, width = w.shape
    blocks = units // BLOCK
    span = width // NX
    wide = span // NC

    def kernel(core_ref, w_ref, o_ref, buf_ref, sem):
        half = 1 - core_ref[0] if other else core_ref[0]
        base = 0 if other else half * blocks
        start = pl.multiple_of(half * wide, wide)

        def fetch(e, x):
            source = w_ref.at[first + e, :, pl.ds(x * span + start, wide)]
            return pltpu.make_async_copy(source, buf_ref.at[e, x], sem.at[e, x])

        for e in range(count):
            for x in range(NX):
                fetch(e, x).start()
        for e in range(count):
            for h in range(NX // 2):
                for t in range(2):
                    fetch(e, 2 * h + t).wait()
                for j in range(blocks):
                    rows = slice(j * BLOCK, (j + 1) * BLOCK)
                    for a in range(SLICES // 2):
                        lanes = slice(a * LANE, (a + 1) * LANE)
                        pair = halves(*[buf_ref[e, 2 * h + t, rows, lanes] for t in range(2)])
                        for b in range(2):
                            o_ref[base + j, 2 * a + b, e, :, h * LANE:(h + 1) * LANE] = pair[b]

    shape = (blocks if other else NC * blocks, SLICES, count, BLOCK, COLS)
    return pl.pallas_call(
        kernel,
        compiler_params=LARGE if other else MEDIUM,
        in_specs=[SMEM, pl.BlockSpec(memory_space=pltpu.HBM)],
        out_specs=VMEM,
        out_shape=jax.ShapeDtypeStruct(shape, w.dtype),
        scratch_shapes=[pltpu.VMEM((count, NX, units, wide), w.dtype), pltpu.SemaphoreType.DMA((count, NX))],
    )(core, w)


def join_kernel(core_ref, *refs):
    got_refs, (_, o_ref, sem) = refs[:PIECES], refs[PIECES:]
    blocks, _, count = got_refs[0].shape[:3]
    copies = []
    for k, got_ref in enumerate(got_refs):
        target = o_ref.at[pl.ds((1 - core_ref[0]) * blocks, blocks), :, pl.ds(k * count, count)]
        copies.append(pltpu.make_async_copy(got_ref, target, sem.at[k]))
    for copy in copies:
        copy.start()
    for copy in copies:
        copy.wait()


def join(core, got, held):
    return pl.pallas_call(
        join_kernel,
        compiler_params=SMALL,
        in_specs=[SMEM] + [ANY] * (PIECES + 1),
        out_specs=ANY,
        out_shape=jax.ShapeDtypeStruct(held.shape, held.dtype),
        scratch_shapes=[pltpu.SemaphoreType.DMA((PIECES,))],
        input_output_aliases={1 + PIECES: 0},
    )(core, *got, held)


def grams(anchor_of, core, columns, other):
    def kernel(anchor_ref, core_ref, w_ref, o_ref):
        half = 1 - core_ref[0] if other else core_ref[0]

        def step(g, carry):
            parts = []
            for i in range(PACK):
                p = (half * GROUPS + g) * PACK + i
                lead = flip(anchor_ref[flip(p)])
                parts.append(lax.dot_general(w_ref[lead], w_ref[p], NT, preferred_element_type=jnp.float32))
            o_ref[g] = jnp.concatenate(parts, axis=1)
            return carry

        lax.fori_loop(0, GROUPS, step, 0, unroll=4)

    return pl.pallas_call(
        kernel,
        compiler_params=SMALL,
        in_specs=[SMEM, SMEM, VMEM],
        out_specs=VMEM,
        out_shape=jax.ShapeDtypeStruct((GROUPS, BLOCK, LANES), jnp.float32),
    )(anchor_of, core, columns)


def split(value):
    high = value.astype(jnp.bfloat16)
    return high, (value - high.astype(jnp.float32)).astype(jnp.bfloat16)


def fold(product):
    return product[:BLOCK, :LANE] + product[BLOCK:, :LANE] + product[:BLOCK, LANE:]


def polar_kernel(part_ref, o_ref, x_ref):
    count = MINE * PACK
    for g in range(MINE):
        total = part_ref[0, g]
        for s in range(1, SLICES):
            total = total + part_ref[s, g]
        total = total * (1.0 / SCALE)
        for i in range(PACK):
            gram = total[:, i * BLOCK:(i + 1) * BLOCK]
            gram = jnp.concatenate([gram, jnp.zeros((BLOCK, LANE - BLOCK), jnp.float32)], axis=1)
            norm = jnp.sqrt(jnp.sum(jnp.sum(gram * gram, axis=1, keepdims=True), axis=0, keepdims=True) + 1e-06)
            x_ref[g * PACK + i] = gram / norm
    pad = jnp.zeros((LANE - BLOCK, LANE), jnp.bfloat16)

    def square(high, low):
        return lax.dot_general(
            jnp.concatenate([high, low], 0), jnp.concatenate([high, pad, low, pad], 0), NT,
            preferred_element_type=jnp.float32,
        )

    def times(one, two):
        wide = jnp.concatenate([jnp.concatenate([part, pad], 0) for part in two], 1)
        return jnp.dot(jnp.concatenate(one, 0), wide, preferred_element_type=jnp.float32)

    def step(it, carry):
        values = [x_ref[n] for n in range(count)]
        halves = [split(v) for v in values]
        squares = [split(fold(square(*v))) for v in halves]
        cubes = [times(s, v) for s, v in zip(squares, halves)]
        for n in range(count):
            x_ref[n] = 1.5 * values[n] - 0.5 * fold(cubes[n])
        return carry

    lax.fori_loop(0, NS_STEPS, step, 0)
    for g in range(MINE):
        packed = jnp.concatenate([x_ref[g * PACK + i][:, :BLOCK] for i in range(PACK)], axis=1).astype(o_ref.dtype)
        for s in range(SLICES):
            o_ref[s, g] = packed


def polars(parts):
    return pl.pallas_call(
        polar_kernel,
        compiler_params=SMALL,
        in_specs=[VMEM],
        out_specs=VMEM,
        out_shape=jax.ShapeDtypeStruct((SLICES, MINE, BLOCK, LANES), jnp.bfloat16),
        scratch_shapes=[pltpu.VMEM((MINE * PACK, BLOCK, LANE), jnp.float32)],
    )(parts)


def turn(cluster_ref, weight_ref, polar_ref, w_ref, acc_ref, half):
    def step(g, carry):
        packed = polar_ref[g]
        turned = []
        for i in range(PACK):
            p = (half * GROUPS + g) * PACK + i
            part = jnp.dot(packed[:, i * BLOCK:(i + 1) * BLOCK], w_ref[p], preferred_element_type=jnp.float32)
            turned.append((part * weight_ref[flip(p)]).astype(jnp.bfloat16).astype(jnp.float32))
        for i in range(PACK):
            k = cluster_ref[flip((half * GROUPS + g) * PACK + i)]
            acc_ref[k] = acc_ref[k] + turned[i]
        return carry

    lax.fori_loop(0, GROUPS, step, 0, unroll=8)


def align_own_kernel(cluster_ref, weight_ref, core_ref, own_ref, w_ref, acc_ref):
    acc_ref[...] = jnp.zeros_like(acc_ref)
    turn(cluster_ref, weight_ref, own_ref, w_ref, acc_ref, core_ref[0])


def align_own(cluster_ids, weight, core, own, columns):
    return pl.pallas_call(
        align_own_kernel,
        compiler_params=SMALL,
        in_specs=[SMEM, SMEM, SMEM, VMEM, VMEM],
        out_specs=VMEM,
        out_shape=jax.ShapeDtypeStruct((CLUSTERS, BLOCK, COLS), jnp.float32),
    )(cluster_ids, weight, core, own, columns)


def align_got_kernel(cluster_ref, weight_ref, core_ref, got_ref, w_ref, sum_ref, o_ref, acc_ref):
    acc_ref[...] = sum_ref[...]
    turn(cluster_ref, weight_ref, got_ref, w_ref, acc_ref, 1 - core_ref[0])
    rows = BLOCK // 2

    def put(k, carry):
        slot = k % (NZB * NZC) * NY + k // (NZB * NZC)
        for h in range(NX // 2):
            pair = halves(*[acc_ref[k, r * rows:(r + 1) * rows, h * LANE:(h + 1) * LANE] for r in range(2)])
            for t in range(2):
                o_ref[slot, 2 * h + t] = pair[t].astype(o_ref.dtype)
        return carry

    lax.fori_loop(0, CLUSTERS, put, 0, unroll=2)


def align_got(cluster_ids, weight, core, got, columns, sums):
    return pl.pallas_call(
        align_got_kernel,
        compiler_params=SMALL,
        in_specs=[SMEM, SMEM, SMEM, VMEM, VMEM, VMEM],
        out_specs=VMEM,
        out_shape=jax.ShapeDtypeStruct((CLUSTERS, NX, BLOCK // 2, LANE), jnp.bfloat16),
        scratch_shapes=[pltpu.VMEM((CLUSTERS, BLOCK, COLS), jnp.float32)],
    )(cluster_ids, weight, core, got, columns, sums)


def final_kernel(m_ref, o_ref, buf_ref, sem):
    rows = NZB * BLOCK

    def put(x):
        return pltpu.make_async_copy(buf_ref.at[x % 2], o_ref.at[0, pl.ds(x * rows, rows)], sem.at[x % 2])

    for x in range(NX):
        if x >= 2:
            put(x - 2).wait()
        for zb in range(NZB):
            for y in range(NY):
                pair = halves(m_ref[zb, 0, y, x], m_ref[zb, 1, y, x])
                buf_ref[x % 2, zb * BLOCK:(zb + 1) * BLOCK, y * LANE:(y + 1) * LANE] = jnp.concatenate(pair, 0)
        put(x).start()
    for x in range(NX - 2, NX):
        put(x).wait()


def final(merged):
    rows = NZB * BLOCK
    width = NC * COLS
    return pl.pallas_call(
        final_kernel,
        compiler_params=SMALL,
        in_specs=[VMEM],
        out_specs=ANY,
        out_shape=jax.ShapeDtypeStruct((1, NX * rows, width), merged.dtype),
        scratch_shapes=[pltpu.VMEM((2, rows, width), merged.dtype), pltpu.SemaphoreType.DMA((2,))],
    )(merged)


def exchange(value, axes):
    return lax.all_to_all(value, axes, split_axis=0, concat_axis=0, tiled=True)


def on_device(w_up, cluster, counts):
    cluster_ids = cluster[:, 0]
    index = jnp.arange(EXPERTS, dtype=jnp.int32)
    labels = jnp.arange(CLUSTERS, dtype=jnp.int32)
    member = cluster_ids[None, :] == labels[:, None]
    score = counts * EXPERTS + (EXPERTS - 1 - index)
    best = jnp.max(jnp.where(member, score[None, :], -1), axis=1)
    leader = EXPERTS - 1 - best % EXPERTS
    anchor_of = jnp.sum(jnp.where(member, leader[:, None], 0), axis=0)
    total = jnp.sum(jnp.where(member, counts[None, :], 0), axis=1).astype(jnp.float32)
    weight = counts.astype(jnp.float32) / jnp.sum(jnp.where(member, total[:, None], 0.0), axis=0)
    core = lax.axis_index("core").astype(jnp.int32).reshape(1)

    experts = w_up.shape[0]
    count = experts // PIECES
    sent = [spread(core, w_up, True, k * count, count) for k in range(PIECES)]
    got = [lax.ppermute(piece, "core", SWAP) for piece in sent]
    rows = join(core, got, spread(core, w_up, False, 0, experts))
    rows = rows.reshape(NZB * SLICES, -1, COLS)
    rows, anchor_of, weight = lax.optimization_barrier((rows, anchor_of, weight))
    columns = exchange(rows, ("zb", "y", "zc")).reshape(EXPERTS, BLOCK, COLS)

    send = (grams(anchor_of, core, columns, True) * SCALE).astype(jnp.float16)
    got = lax.ppermute(send, "core", SWAP).astype(jnp.float32)
    partial = (grams(anchor_of, core, columns, False) * SCALE + got).astype(jnp.float16)
    parts = exchange(partial, ("zc", "y")).astype(jnp.float32)
    copies = polars(parts.reshape(SLICES, MINE, BLOCK, LANES))
    own = exchange(copies, ("zc", "y")).reshape(GROUPS, BLOCK, LANES)
    got = lax.ppermute(own, "core", SWAP)
    merged = align_got(cluster_ids, weight, core, got, columns, align_own(cluster_ids, weight, core, own, columns))

    merged = exchange(merged.reshape(-1, BLOCK // 2, LANE), ("zb", "zc", "y", "x"))
    return final(merged.reshape(NZB, NZC, NY, NX, BLOCK // 2, LANE))


def solution(mesh):
    grid = Mesh(mesh.devices.reshape(NY, NZB, NZC, NX, NC), ("y", "zb", "zc", "x", "core"))
    return jax.shard_map(
        on_device,
        mesh=grid,
        in_specs=(P(("y", "zb", "zc"), ("x", "core"), None), P(), P()),
        out_specs=P(("y", "zb", "zc"), None, ("x", "core")),
        check_vma=False,
    )
```

```python
import jax
import jax.numpy as jnp
from jax import lax
from jax.experimental import pallas as pl
from jax.experimental.pallas import tpu as pltpu
from jax.sharding import Mesh, PartitionSpec as P

BLOCK = 96
NS_STEPS = 8
NY, NZB, NZC, NX, NC = 4, 4, 2, 4, 2
EXPERTS = 128
CLUSTERS = 32
COLS = 256
PACK = 4
LANE = 128
LANES = PACK * BLOCK
SLICES = NY * NZC
SCALE = 8192.0
PIECES = 2
GROUPS = EXPERTS // PACK // NC
MINE = GROUPS // SLICES
SWAP = [(0, 1), (1, 0)]
VMEM = pl.BlockSpec(memory_space=pltpu.VMEM)
SMEM = pl.BlockSpec(memory_space=pltpu.SMEM)
ANY = pl.BlockSpec(memory_space=pl.ANY)
NT = (((1,), (1,)), ((), ()))
MEDIUM = pltpu.CompilerParams(vmem_limit_bytes=46 * 2**20)
LARGE = pltpu.CompilerParams(vmem_limit_bytes=58 * 2**20)
SMALL = pltpu.CompilerParams(vmem_limit_bytes=20 * 2**20)


def flip(position):
    return ((position >> 3) & 3) * 32 + (position >> 5) * 8 + (position & 7)


def halves(first, second):
    low = lax.broadcasted_iota(jnp.int32, first.shape, 1) < LANE // 2
    return (
        jnp.where(low, first, pltpu.roll(second, LANE // 2, 1)),
        jnp.where(low, pltpu.roll(first, LANE // 2, 1), second),
    )


def spread(core, w, other, first, count):
    experts, units, width = w.shape
    blocks = units // BLOCK
    span = width // NX
    wide = span // NC

    def kernel(core_ref, w_ref, o_ref, buf_ref, sem):
        half = 1 - core_ref[0] if other else core_ref[0]
        base = 0 if other else half * blocks
        start = pl.multiple_of(half * wide, wide)

        def fetch(e, x):
            source = w_ref.at[first + e, :, pl.ds(x * span + start, wide)]
            return pltpu.make_async_copy(source, buf_ref.at[e, x], sem.at[e, x])

        for e in range(count):
            for x in range(NX):
                fetch(e, x).start()
        for e in range(count):
            for h in range(NX // 2):
                for t in range(2):
                    fetch(e, 2 * h + t).wait()
                for j in range(blocks):
                    rows = slice(j * BLOCK, (j + 1) * BLOCK)
                    for a in range(SLICES // 2):
                        lanes = slice(a * LANE, (a + 1) * LANE)
                        pair = halves(*[buf_ref[e, 2 * h + t, rows, lanes] for t in range(2)])
                        for b in range(2):
                            o_ref[base + j, 2 * a + b, e, :, h * LANE:(h + 1) * LANE] = pair[b]

    shape = (blocks if other else NC * blocks, SLICES, count, BLOCK, COLS)
    return pl.pallas_call(
        kernel,
        compiler_params=LARGE if other else MEDIUM,
        in_specs=[SMEM, pl.BlockSpec(memory_space=pltpu.HBM)],
        out_specs=VMEM,
        out_shape=jax.ShapeDtypeStruct(shape, w.dtype),
        scratch_shapes=[pltpu.VMEM((count, NX, units, wide), w.dtype), pltpu.SemaphoreType.DMA((count, NX))],
    )(core, w)


def join_kernel(core_ref, *refs):
    got_refs, (_, o_ref, sem) = refs[:PIECES], refs[PIECES:]
    blocks, _, count = got_refs[0].shape[:3]
    copies = []
    for k, got_ref in enumerate(got_refs):
        target = o_ref.at[pl.ds((1 - core_ref[0]) * blocks, blocks), :, pl.ds(k * count, count)]
        copies.append(pltpu.make_async_copy(got_ref, target, sem.at[k]))
    for copy in copies:
        copy.start()
    for copy in copies:
        copy.wait()


def join(core, got, held):
    return pl.pallas_call(
        join_kernel,
        compiler_params=SMALL,
        in_specs=[SMEM] + [ANY] * (PIECES + 1),
        out_specs=ANY,
        out_shape=jax.ShapeDtypeStruct(held.shape, held.dtype),
        scratch_shapes=[pltpu.SemaphoreType.DMA((PIECES,))],
        input_output_aliases={1 + PIECES: 0},
    )(core, *got, held)


def grams(anchor_of, core, columns, other):
    def kernel(anchor_ref, core_ref, w_ref, o_ref):
        half = 1 - core_ref[0] if other else core_ref[0]

        def step(g, carry):
            parts = []
            for i in range(PACK):
                p = (half * GROUPS + g) * PACK + i
                lead = flip(anchor_ref[flip(p)])
                parts.append(lax.dot_general(w_ref[lead], w_ref[p], NT, preferred_element_type=jnp.float32))
            o_ref[g] = jnp.concatenate(parts, axis=1)
            return carry

        lax.fori_loop(0, GROUPS, step, 0, unroll=8)

    return pl.pallas_call(
        kernel,
        compiler_params=SMALL,
        in_specs=[SMEM, SMEM, VMEM],
        out_specs=VMEM,
        out_shape=jax.ShapeDtypeStruct((GROUPS, BLOCK, LANES), jnp.float32),
    )(anchor_of, core, columns)


def split(value):
    high = value.astype(jnp.bfloat16)
    return high, (value - high.astype(jnp.float32)).astype(jnp.bfloat16)


def fold(product):
    return product[:BLOCK, :LANE] + product[BLOCK:, :LANE] + product[:BLOCK, LANE:]


def polar_kernel(part_ref, o_ref, x_ref):
    count = MINE * PACK
    for g in range(MINE):
        total = part_ref[0, g]
        for s in range(1, SLICES):
            total = total + part_ref[s, g]
        total = total * (1.0 / SCALE)
        for i in range(PACK):
            gram = total[:, i * BLOCK:(i + 1) * BLOCK]
            gram = jnp.concatenate([gram, jnp.zeros((BLOCK, LANE - BLOCK), jnp.float32)], axis=1)
            norm = jnp.sqrt(jnp.sum(jnp.sum(gram * gram, axis=1, keepdims=True), axis=0, keepdims=True) + 1e-06)
            x_ref[g * PACK + i] = gram / norm
    pad = jnp.zeros((LANE - BLOCK, LANE), jnp.bfloat16)

    def square(high, low):
        return lax.dot_general(
            jnp.concatenate([high, low], 0), jnp.concatenate([high, pad, low, pad], 0), NT,
            preferred_element_type=jnp.float32,
        )

    def times(one, two):
        wide = jnp.concatenate([jnp.concatenate([part, pad], 0) for part in two], 1)
        return jnp.dot(jnp.concatenate(one, 0), wide, preferred_element_type=jnp.float32)

    def step(it, carry):
        values = [x_ref[n] for n in range(count)]
        halves = [split(v) for v in values]
        squares = [split(fold(square(*v))) for v in halves]
        cubes = [times(s, v) for s, v in zip(squares, halves)]
        for n in range(count):
            x_ref[n] = 1.5 * values[n] - 0.5 * fold(cubes[n])
        return carry

    lax.fori_loop(0, NS_STEPS, step, 0)
    for g in range(MINE):
        packed = jnp.concatenate([x_ref[g * PACK + i][:, :BLOCK] for i in range(PACK)], axis=1).astype(o_ref.dtype)
        for s in range(SLICES):
            o_ref[s, g] = packed


def polars(parts):
    return pl.pallas_call(
        polar_kernel,
        compiler_params=SMALL,
        in_specs=[VMEM],
        out_specs=VMEM,
        out_shape=jax.ShapeDtypeStruct((SLICES, MINE, BLOCK, LANES), jnp.bfloat16),
        scratch_shapes=[pltpu.VMEM((MINE * PACK, BLOCK, LANE), jnp.float32)],
    )(parts)


def turn(cluster_ref, weight_ref, polar_ref, w_ref, acc_ref, half):
    def step(g, carry):
        packed = polar_ref[g]
        turned = []
        for i in range(PACK):
            p = (half * GROUPS + g) * PACK + i
            part = jnp.dot(packed[:, i * BLOCK:(i + 1) * BLOCK], w_ref[p], preferred_element_type=jnp.float32)
            turned.append((part * weight_ref[flip(p)]).astype(jnp.bfloat16).astype(jnp.float32))
        for i in range(PACK):
            k = cluster_ref[flip((half * GROUPS + g) * PACK + i)]
            acc_ref[k] = acc_ref[k] + turned[i]
        return carry

    lax.fori_loop(0, GROUPS, step, 0, unroll=8)


def align_own_kernel(cluster_ref, weight_ref, core_ref, own_ref, w_ref, acc_ref):
    acc_ref[...] = jnp.zeros_like(acc_ref)
    turn(cluster_ref, weight_ref, own_ref, w_ref, acc_ref, core_ref[0])


def align_own(cluster_ids, weight, core, own, columns):
    return pl.pallas_call(
        align_own_kernel,
        compiler_params=SMALL,
        in_specs=[SMEM, SMEM, SMEM, VMEM, VMEM],
        out_specs=VMEM,
        out_shape=jax.ShapeDtypeStruct((CLUSTERS, BLOCK, COLS), jnp.float32),
    )(cluster_ids, weight, core, own, columns)


def align_got_kernel(cluster_ref, weight_ref, core_ref, got_ref, w_ref, sum_ref, o_ref, acc_ref):
    acc_ref[...] = sum_ref[...]
    turn(cluster_ref, weight_ref, got_ref, w_ref, acc_ref, 1 - core_ref[0])
    rows = BLOCK // 2

    def put(k, carry):
        slot = k % (NZB * NZC) * NY + k // (NZB * NZC)
        for h in range(NX // 2):
            pair = halves(*[acc_ref[k, r * rows:(r + 1) * rows, h * LANE:(h + 1) * LANE] for r in range(2)])
            for t in range(2):
                o_ref[slot, 2 * h + t] = pair[t].astype(o_ref.dtype)
        return carry

    lax.fori_loop(0, CLUSTERS, put, 0, unroll=2)


def align_got(cluster_ids, weight, core, got, columns, sums):
    return pl.pallas_call(
        align_got_kernel,
        compiler_params=SMALL,
        in_specs=[SMEM, SMEM, SMEM, VMEM, VMEM, VMEM],
        out_specs=VMEM,
        out_shape=jax.ShapeDtypeStruct((CLUSTERS, NX, BLOCK // 2, LANE), jnp.bfloat16),
        scratch_shapes=[pltpu.VMEM((CLUSTERS, BLOCK, COLS), jnp.float32)],
    )(cluster_ids, weight, core, got, columns, sums)


def final_kernel(m_ref, o_ref, buf_ref, sem):
    rows = NZB * BLOCK

    def put(x):
        return pltpu.make_async_copy(buf_ref.at[x % 2], o_ref.at[0, pl.ds(x * rows, rows)], sem.at[x % 2])

    for x in range(NX):
        if x >= 2:
            put(x - 2).wait()
        for zb in range(NZB):
            for y in range(NY):
                pair = halves(m_ref[zb, 0, y, x], m_ref[zb, 1, y, x])
                buf_ref[x % 2, zb * BLOCK:(zb + 1) * BLOCK, y * LANE:(y + 1) * LANE] = jnp.concatenate(pair, 0)
        put(x).start()
    for x in range(NX - 2, NX):
        put(x).wait()


def final(merged):
    rows = NZB * BLOCK
    width = NC * COLS
    return pl.pallas_call(
        final_kernel,
        compiler_params=SMALL,
        in_specs=[VMEM],
        out_specs=ANY,
        out_shape=jax.ShapeDtypeStruct((1, NX * rows, width), merged.dtype),
        scratch_shapes=[pltpu.VMEM((2, rows, width), merged.dtype), pltpu.SemaphoreType.DMA((2,))],
    )(merged)


def exchange(value, axes):
    return lax.all_to_all(value, axes, split_axis=0, concat_axis=0, tiled=True)


def on_device(w_up, cluster, counts):
    cluster_ids = cluster[:, 0]
    index = jnp.arange(EXPERTS, dtype=jnp.int32)
    labels = jnp.arange(CLUSTERS, dtype=jnp.int32)
    member = cluster_ids[None, :] == labels[:, None]
    score = counts * EXPERTS + (EXPERTS - 1 - index)
    best = jnp.max(jnp.where(member, score[None, :], -1), axis=1)
    leader = EXPERTS - 1 - best % EXPERTS
    anchor_of = jnp.sum(jnp.where(member, leader[:, None], 0), axis=0)
    total = jnp.sum(jnp.where(member, counts[None, :], 0), axis=1).astype(jnp.float32)
    weight = counts.astype(jnp.float32) / jnp.sum(jnp.where(member, total[:, None], 0.0), axis=0)
    core = lax.axis_index("core").astype(jnp.int32).reshape(1)

    experts = w_up.shape[0]
    count = experts // PIECES
    sent = [spread(core, w_up, True, k * count, count) for k in range(PIECES)]
    got = [lax.ppermute(piece, "core", SWAP) for piece in sent]
    rows = join(core, got, spread(core, w_up, False, 0, experts))
    rows = rows.reshape(NZB * SLICES, -1, COLS)
    rows, anchor_of, weight = lax.optimization_barrier((rows, anchor_of, weight))
    columns = exchange(rows, ("zb", "y", "zc")).reshape(EXPERTS, BLOCK, COLS)

    send = (grams(anchor_of, core, columns, True) * SCALE).astype(jnp.float16)
    got = lax.ppermute(send, "core", SWAP).astype(jnp.float32)
    partial = (grams(anchor_of, core, columns, False) * SCALE + got).astype(jnp.float16)
    parts = exchange(partial, ("zc", "y")).astype(jnp.float32)
    copies = polars(parts.reshape(SLICES, MINE, BLOCK, LANES))
    own = exchange(copies, ("zc", "y")).reshape(GROUPS, BLOCK, LANES)
    got = lax.ppermute(own, "core", SWAP)
    merged = align_got(cluster_ids, weight, core, got, columns, align_own(cluster_ids, weight, core, own, columns))

    merged = exchange(merged.reshape(-1, BLOCK // 2, LANE), ("zb", "zc", "y", "x"))
    return final(merged.reshape(NZB, NZC, NY, NX, BLOCK // 2, LANE))


def solution(mesh):
    grid = Mesh(mesh.devices.reshape(NY, NZB, NZC, NX, NC), ("y", "zb", "zc", "x", "core"))
    return jax.shard_map(
        on_device,
        mesh=grid,
        in_specs=(P(("y", "zb", "zc"), ("x", "core"), None), P(), P()),
        out_specs=P(("y", "zb", "zc"), None, ("x", "core")),
        check_vma=False,
    )
```
